32 devices in a mesh: gx: 8 (over z, y), gy: 2 (over x), gz: 2 (over core).
Axes of the slice: x: 2, y: 2, z: 4, core: 2. Of those that a mesh axis runs over, the one named last changes fastest.
Arguments:
- tensor_blocks: bfloat16 [8, 2, 2, 2, 128, 128, 128], P('gx', 'gy', 'gz'), may hold values from -768 to 768
- block_coords: int32 [8, 2, 2, 2, 3], P('gx', 'gy', 'gz'), may hold values from 0 to 1, as said below
- live_counts: int32 [8, 2, 2], P('gx', 'gy', 'gz'), may hold values from 1 to 2, as said below
- factor_a: bfloat16 [8, 256, 256], P('gx', ('gy', 'gz')), may hold values from 0.049804688 to 1
- factor_b: bfloat16 [2, 256, 256], P('gy', ('gx', 'gz')), may hold values from 0.049804688 to 1
- factor_c: bfloat16 [2, 256, 256], P('gz', ('gx', 'gy')), may hold values from 0.049804688 to 1
Outputs:
- updated_a: bfloat16 [8, 256, 256], P('gx', ('gy', 'gz'))
- updated_b: bfloat16 [2, 256, 256], P('gy', ('gx', 'gz'))
- updated_c: bfloat16 [2, 256, 256], P('gz', ('gx', 'gy'))
The draws below stay inside these ranges and needn't reach their ends.
Inputs may be any that keep to these rules, and one draw needn't show every extreme that they name: `block_coords`: within one cell the 2 slots hold distinct positions. `live_counts`: some cell has exactly 2 live slots and another exactly one.
All inputs are finite; a program needn't handle non-finite values. Where the reference program divides by a largest or mean magnitude, that divisor is 1e-20 or more.
Results may differ from the reference program's by a relative error of at most 0.0055.
Values may be sent and summed in bfloat16 or wider, within the bound.
No kernel may reach another device: no remote copies, remote signals or barrier semaphores. Data moves between devices by JAX's collectives and lax.ppermute only.
A program may use at most 256 MiB of HBM per device.

```python
import jax
import jax.numpy as jnp
from jax import lax

R = 256
BS = 128
CB = 2
NB_DEV = 2
NS_STEPS = 8
ADMM_ITERS = 4
SLAB = 256
N_GX = 8
N_GY = 2
N_GZ = 2


def draw_block_coords(key, part):
    devices = N_GX * N_GY * N_GZ
    key_list = jax.random.split(key, devices)

    def pick_slots(subkey):
        return jax.random.permutation(subkey, CB * CB * CB)[:NB_DEV]
    chosen = jax.vmap(pick_slots)(key_list)
    triples = jnp.stack([chosen // (CB * CB), chosen // CB % CB, chosen % CB], axis=-1)
    return triples.reshape(N_GX, N_GY, N_GZ, NB_DEV, 3).astype(jnp.int32)


def draw_live_counts(key, part):
    devices = N_GX * N_GY * N_GZ
    counts = jax.random.randint(jax.random.fold_in(key, 11), (devices,), 1, NB_DEV + 1)
    shuffle = jax.random.permutation(jax.random.fold_in(key, 12), devices)
    counts = counts.at[shuffle[0]].set(NB_DEV).at[shuffle[1]].set(1)
    return counts.reshape(N_GX, N_GY, N_GZ).astype(jnp.int32)


def block_scale(key, shape, cuts, low, largest):
    factor_of = 1.0
    for axis_at, blocks in cuts:
        draws = jax.random.uniform(jax.random.fold_in(jax.random.fold_in(key, 6), axis_at), (blocks,), jnp.float32, low / len(cuts), largest / len(cuts))
        factor_of = factor_of * jnp.repeat(jnp.exp(draws), shape[axis_at] // blocks).reshape((-1,) + (1,) * (len(shape) - 1 - axis_at))
    return factor_of


def noise(rng, extent, spread, most, cuts=(), kind=jnp.bfloat16):
    loudness = block_scale(rng, extent, cuts, -0.22, 0.18) if cuts else 1.0
    values = jax.random.normal(rng, extent, jnp.float32) * spread * loudness
    return jnp.minimum(jnp.maximum(values, -most), most).astype(kind)


def setup_inputs(seed: int = 0) -> dict:
    splits = jax.random.split(jax.random.key(seed), 7)
    return {
        "tensor_blocks": noise(splits[0], (N_GX, N_GY, N_GZ, NB_DEV, BS, BS, BS), (CB * CB * BS * N_GY * N_GZ // 16), 768.0, ((0, 8), (1, 2), (2, 2))),
        "block_coords": draw_block_coords(jax.random.fold_in(splits[6], 71), 0),
        "live_counts": draw_live_counts(jax.random.fold_in(splits[6], 71), 0),
        "factor_a": jnp.clip(0.049804688 + 0.9501953 * jax.random.uniform(splits[3], (N_GX, SLAB, R), jnp.float32) ** block_scale(splits[3], (N_GX, SLAB, R), ((0, 8), (1, 4)), -0.2, 0.2), 0.049804688, 1.0).astype(jnp.bfloat16),
        "factor_b": jnp.clip(0.049804688 + 0.9501953 * jax.random.uniform(splits[4], (N_GY, SLAB, R), jnp.float32) ** block_scale(splits[4], (N_GY, SLAB, R), ((0, 2), (1, 16)), -0.2, 0.2), 0.049804688, 1.0).astype(jnp.bfloat16),
        "factor_c": jnp.clip(0.049804688 + 0.9501953 * jax.random.uniform(splits[5], (N_GZ, SLAB, R), jnp.float32) ** block_scale(splits[5], (N_GZ, SLAB, R), ((0, 2), (1, 16)), -0.2, 0.2), 0.049804688, 1.0).astype(jnp.bfloat16),
    }


HIGHEST = lax.Precision.HIGHEST


def gram_rows(factor):
    return lax.dot_general(factor, factor, (((0,), (0,)), ((), ())), preferred_element_type=jnp.float32)


def newton_inverse(gram_left, gram_right):
    weighted = gram_left * gram_right
    width = weighted.shape[0]
    identity = jnp.eye(width, dtype=weighted.dtype)
    penalty = jnp.trace(weighted) / width
    system = weighted + penalty * identity
    bound = jnp.max(jnp.sum(jnp.abs(system), axis=1))
    inverse = identity / bound
    for step in range(NS_STEPS):
        inverse = jnp.dot(inverse, 2.0 * identity - jnp.dot(system, inverse, precision=HIGHEST), precision=HIGHEST)
    return penalty, inverse


def split_updates(totals, start, penalty, inverse):
    primal = start.astype(jnp.float32)
    dual = jnp.zeros_like(primal)
    for step in range(ADMM_ITERS):
        target = jnp.dot(totals + penalty * (primal + dual), inverse, precision=HIGHEST)
        primal = jnp.maximum(target - dual, 0.0)
        dual = dual + primal - target
    return primal.astype(jnp.bfloat16)


def walk(tensor_blocks, block_coords, live_counts, running, contribution):
    slot_count = tensor_blocks.shape[3]
    side = tensor_blocks.shape[4]
    flat = tensor_blocks.reshape(-1, side, side, side)
    triples = block_coords.reshape(-1, 3)
    counts = live_counts.reshape(-1)
    slab = CB * side

    def visit(position, totals):
        block = lax.dynamic_index_in_dim(flat, position, 0, keepdims=False)
        triple = lax.dynamic_index_in_dim(triples, position, 0, keepdims=False)
        device = position // slot_count
        slot = position % slot_count
        grid_x = device // (N_GY * N_GZ)
        grid_y = (device // N_GZ) % N_GY
        grid_z = device % N_GZ
        starts = ((grid_x * slab + triple[0] * side).astype(jnp.int32),
                  (grid_y * slab + triple[1] * side).astype(jnp.int32),
                  (grid_z * slab + triple[2] * side).astype(jnp.int32))
        target, terms = contribution(block, starts)
        weight = (slot < counts[device]).astype(jnp.float32)
        current = lax.dynamic_slice_in_dim(totals, target, side, 0)
        return lax.dynamic_update_slice_in_dim(totals, current + weight * terms, target, 0)

    return lax.fori_loop(0, flat.shape[0], visit, running)


def reference(tensor_blocks, block_coords, live_counts, factor_a, factor_b, factor_c):
    width = factor_a.shape[2]
    side = tensor_blocks.shape[4]
    full_a = factor_a.reshape(-1, width)
    full_b = factor_b.reshape(-1, width)
    full_c = factor_c.reshape(-1, width)
    gram_b = gram_rows(full_b)
    gram_c = gram_rows(full_c)

    def first_terms(block, starts):
        band_b = lax.dynamic_slice_in_dim(full_b, starts[1], side, 0)
        band_c = lax.dynamic_slice_in_dim(full_c, starts[2], side, 0)
        contracted = jnp.dot(block.reshape(side * side, side), band_c, preferred_element_type=jnp.float32).reshape(side, side, width)
        return starts[0], jnp.sum(contracted * band_b.astype(jnp.float32)[None], axis=1)

    sums_a = walk(tensor_blocks, block_coords, live_counts, jnp.zeros((full_a.shape[0], width), jnp.float32), first_terms)
    penalty, inverse = newton_inverse(gram_b, gram_c)
    new_a = split_updates(sums_a, full_a, penalty, inverse)
    gram_a = gram_rows(new_a)

    def project(block, starts):
        band_a = lax.dynamic_slice_in_dim(new_a, starts[0], side, 0)
        projected = lax.dot_general(band_a, block.reshape(side, side * side), (((0,), (0,)), ((), ())), preferred_element_type=jnp.float32)
        return projected.reshape(width, side, side)

    def second_terms(block, starts):
        band_c = lax.dynamic_slice_in_dim(full_c, starts[2], side, 0)
        projected = project(block, starts)
        return starts[1], jnp.sum(projected * band_c.astype(jnp.float32).T[:, None, :], axis=2).T

    sums_b = walk(tensor_blocks, block_coords, live_counts, jnp.zeros((full_b.shape[0], width), jnp.float32), second_terms)
    penalty, inverse = newton_inverse(gram_a, gram_c)
    new_b = split_updates(sums_b, full_b, penalty, inverse)
    gram_b_new = gram_rows(new_b)

    def third_terms(block, starts):
        band_b = lax.dynamic_slice_in_dim(new_b, starts[1], side, 0)
        projected = project(block, starts)
        return starts[2], jnp.sum(projected * band_b.astype(jnp.float32).T[:, :, None], axis=1).T

    sums_c = walk(tensor_blocks, block_coords, live_counts, jnp.zeros((full_c.shape[0], width), jnp.float32), third_terms)
    penalty, inverse = newton_inverse(gram_a, gram_b_new)
    new_c = split_updates(sums_c, full_c, penalty, inverse)
    return new_a.reshape(factor_a.shape), new_b.reshape(factor_b.shape), new_c.reshape(factor_c.shape)
```

```python
import functools

import jax
import jax.numpy as jnp
from jax import lax
from jax.experimental import pallas as pl
from jax.experimental.pallas import tpu as pltpu
from jax.sharding import PartitionSpec as P

NS_STEPS = 8
ADMM_ITERS = 4

f32 = jnp.float32
bf16 = jnp.bfloat16

ANY = pl.BlockSpec(memory_space=pl.ANY)
VM = pl.BlockSpec(memory_space=pltpu.VMEM)
SM = pl.BlockSpec(memory_space=pltpu.SMEM)


def split(value):
    high = value.astype(bf16)
    return high, (value - high.astype(f32)).astype(bf16)


def dot3(left, right):
    left_high, left_low = split(left)
    right_high, right_low = split(right)
    mul = functools.partial(jnp.dot, preferred_element_type=f32)
    return mul(left_high, right_high) + (mul(left_low, right_high) + mul(left_high, right_low))


def gram_of(rows):
    return lax.dot_general(rows, rows, (((0,), (0,)), ((), ())), preferred_element_type=f32)


def newton_inverse(weighted):
    width = weighted.shape[0]
    row = lax.broadcasted_iota(jnp.int32, weighted.shape, 0)
    col = lax.broadcasted_iota(jnp.int32, weighted.shape, 1)
    identity = (row == col).astype(f32)
    penalty = jnp.sum(weighted * identity) / width
    system = weighted + penalty * identity
    bound = jnp.max(jnp.sum(jnp.abs(system), axis=1))
    scaled = system / bound
    product = 2.0 * identity - scaled
    scaled = 2.0 * scaled - dot3(scaled, scaled)
    for _ in range(NS_STEPS - 2):
        both = dot3(jnp.concatenate([scaled, product], axis=0), scaled)
        scaled = 2.0 * scaled - both[:width]
        product = 2.0 * product - both[width:]
    product = 2.0 * product - dot3(product, scaled)
    return penalty, product / bound


def row_update(sums, start, penalty, inverse):
    primal = start.astype(f32)
    dual = jnp.zeros_like(primal)
    for _ in range(ADMM_ITERS):
        target = dot3(sums + penalty * (primal + dual), inverse)
        primal = jnp.maximum(target - dual, 0.0)
        dual = dual + primal - target
    return primal.astype(bf16)


def contract_body(first, chunk, group, out_axis, coords, live, x_hbm, left_ref, right_ref, out_ref, x_ref, band_ref, acc_ref, sem):
    slots, side = x_hbm.shape[0], x_hbm.shape[1]
    chunks = side // chunk

    def copy(slot, n):
        span = pl.ds(n * chunk, chunk)
        return pltpu.make_async_copy(x_hbm.at[slot, span], x_ref.at[slot, span], sem.at[slot, n])

    for slot in range(slots):

        @pl.when(slot < live[0])
        def _():
            for n in range(chunks):
                copy(slot, n).start()

    out_ref[...] = jnp.zeros_like(out_ref)
    for slot in range(slots):

        @pl.when(slot < live[0])
        def _():
            start = [pl.multiple_of(coords[3 * slot + mode] * side, side) for mode in range(3)]
            if first:
                right = right_ref[pl.ds(start[2], side), :]
                band_ref[...] = left_ref[pl.ds(start[1], side), :].astype(f32)
            else:
                right = right_ref[pl.ds(start[3 - out_axis], side), :]
                band_ref[...] = left_ref[pl.ds(start[0], side), :].astype(f32)
                acc_ref[...] = jnp.zeros_like(acc_ref)
            for n in range(chunks):
                copy(slot, n).wait()
                for g in range(chunk // group):
                    at = n * chunk + g * group
                    block = x_ref[slot, at : at + group]
                    if out_axis == 2:
                        block = jnp.swapaxes(block, 1, 2)
                    terms = jnp.dot(block.reshape(group * side, side), right, preferred_element_type=f32)
                    terms = terms.reshape(group, side, -1)
                    if first:
                        acc_ref[at : at + group, :] = jnp.sum(terms * band_ref[...][None], axis=1)
                    else:
                        acc_ref[...] += jnp.sum(terms * band_ref[at : at + group, :][:, None, :], axis=0)
            out_ref[pl.ds(start[0 if first else out_axis], side), :] += acc_ref[...]


def contract(coords, live, blocks, left, right, out_axis):
    first = out_axis == 0
    slots, side = blocks.shape[0], blocks.shape[1]
    width = left.shape[1]
    chunk = min(64 if out_axis == 2 else 32, side)
    group = min(16, chunk)
    return pl.pallas_call(
        functools.partial(contract_body, first, chunk, group, out_axis),
        in_specs=[SM, SM, ANY, VM, VM],
        out_specs=VM,
        out_shape=jax.ShapeDtypeStruct(left.shape, f32),
        scratch_shapes=[
            pltpu.VMEM(blocks.shape, blocks.dtype),
            pltpu.VMEM((side, width), f32),
            pltpu.VMEM((side, width), f32),
            pltpu.SemaphoreType.DMA((slots, side // chunk)),
        ],
        name=f"contract_{out_axis}",
    )(coords, live, blocks, left, right)


def first_inverse_body(b_ref, c_ref, gram_c_ref, inverse_ref, penalty_ref):
    gram_c = gram_of(c_ref[...])
    gram_c_ref[...] = gram_c
    penalty_ref[0, 0], inverse_ref[...] = newton_inverse(gram_of(b_ref[...]) * gram_c)


def first_inverse(rows_b, rows_c):
    square = jax.ShapeDtypeStruct((rows_b.shape[1],) * 2, f32)
    return pl.pallas_call(
        first_inverse_body,
        out_shape=(square, square, jax.ShapeDtypeStruct((1, 1), f32)),
        out_specs=(VM, VM, SM),
        name="first_inverse",
    )(rows_b, rows_c)


def inverse_body(left_ref, right_ref, inverse_ref, penalty_ref):
    penalty_ref[0, 0], inverse_ref[...] = newton_inverse(left_ref[...] * right_ref[...])


def inverse_of(gram_left, gram_right):
    return pl.pallas_call(
        inverse_body,
        out_shape=(jax.ShapeDtypeStruct(gram_left.shape, f32), jax.ShapeDtypeStruct((1, 1), f32)),
        out_specs=(VM, SM),
        name="inverse",
    )(gram_left, gram_right)


def update_body(sums_ref, start_ref, penalty_ref, inverse_ref, out_ref):
    out_ref[...] = row_update(sums_ref[...], start_ref[...], penalty_ref[0, 0], inverse_ref[...])


def update(sums, start, penalty, inverse):
    return pl.pallas_call(
        update_body,
        in_specs=[VM, VM, SM, VM],
        out_shape=jax.ShapeDtypeStruct(start.shape, bf16),
        out_specs=VM,
        name="update",
    )(sums, start, penalty, inverse)


def gram_body(rows_ref, out_ref):
    out_ref[...] = gram_of(rows_ref[...])


def gram_call(rows):
    return pl.pallas_call(
        gram_body, out_shape=jax.ShapeDtypeStruct((rows.shape[1],) * 2, f32), out_specs=VM, name="gram"
    )(rows)


def on_device(sizes, tensor_blocks, block_coords, live_counts, factor_a, factor_b, factor_c):
    nx, ny, nz = sizes
    x_at, y_at, z_at = (lax.axis_index(name) for name in ("gx", "gy", "gz"))
    slot_count, side = tensor_blocks.shape[3], tensor_blocks.shape[4]
    width = factor_a.shape[2]
    blocks = tensor_blocks.reshape(slot_count, side, side, side)
    coords = block_coords.reshape(slot_count * 3)
    live = live_counts.reshape(1)
    own_a, own_b, own_c = factor_a[0], factor_b[0], factor_c[0]
    rows_a, rows_b, rows_c = own_a.shape[0], own_b.shape[0], own_c.shape[0]
    slab = rows_a * ny * nz

    def pick(array, at, axis=0):
        return lax.dynamic_index_in_dim(array, at, axis, keepdims=False)

    def swap_cores(value):
        return lax.ppermute(value, "gz", [(0, 1), (1, 0)])

    def both_cores(value):
        other = swap_cores(value)
        return jnp.where(z_at == 0, jnp.stack([value, other]), jnp.stack([other, value]))

    def spread(value):
        sent = jnp.broadcast_to(value[None], (nx * ny,) + value.shape)
        got = lax.all_to_all(sent, ("gx", "gy"), 0, 0, tiled=True)
        return got.reshape((nx, ny) + value.shape)

    gathered = both_cores(spread(jnp.concatenate([own_b, own_c], axis=0)))
    full_b = gathered[:, :, :, :rows_b].transpose(2, 1, 0, 3, 4).reshape(ny, slab, width)
    full_c = gathered[:, :, :, rows_b:].reshape(nz, slab, width)
    slab_b, slab_c = pick(full_b, y_at), pick(full_c, z_at)

    partial = contract(coords, live, blocks, slab_b, slab_c, 0).reshape(ny, nz, rows_a, width)
    sums = pick(partial, z_at, 1) + swap_cores(pick(partial, 1 - z_at, 1))
    sums = sums.reshape(ny * rows_a, width)
    gram_c, inverse, penalty = first_inverse(full_b.reshape(ny * slab, width), full_c.reshape(nz * slab, width))
    if ny == 2:
        height = ny * rows_a
        high = lax.reduce_precision(sums, 8, 7)
        sent = jnp.concatenate([high.astype(bf16), (sums - high).astype(bf16), own_a], axis=0)
        got = lax.ppermute(sent, "gy", [(0, 1), (1, 0)])
        sums = (sent[:height].astype(f32) + sent[height : 2 * height].astype(f32)) + (
            got[:height].astype(f32) + got[height : 2 * height].astype(f32)
        )
        other_a = got[2 * height :]
        start_a = jnp.where(y_at == 0, jnp.concatenate([own_a, other_a]), jnp.concatenate([other_a, own_a]))
    else:
        sums = lax.psum(sums, "gy")
        start_a = lax.all_gather(own_a, "gy", axis=0, tiled=True)
    half_a = update(sums, start_a, penalty, inverse)
    slab_a = both_cores(half_a.reshape(ny, rows_a, width)).transpose(1, 0, 2, 3).reshape(slab, width)
    new_a = pick(half_a.reshape(ny, rows_a, width), y_at)

    partial = contract(coords, live, blocks, slab_a, slab_c, 1).reshape(nx, nz, rows_b, width)
    share = width // (ny * nz)
    rows_g = share // nx
    gram_part = lax.dynamic_slice_in_dim(gram_call(slab_a), (y_at * nz + z_at) * share, share, 0)
    sums = pick(partial, z_at, 1) + swap_cores(pick(partial, 1 - z_at, 1))

    def pack(sums_rows, gram_rows):
        return jnp.concatenate([sums_rows, gram_rows], axis=-2)

    def unpack(packed):
        return packed[..., :rows_b, :], packed[..., rows_b:, :]

    got = lax.all_to_all(pack(sums, gram_part.reshape(nx, rows_g, width)), "gx", 0, 0, tiled=True)
    sums, gram_rows = unpack(got)
    gathered = both_cores(spread(pack(jnp.sum(sums, axis=0), jnp.sum(gram_rows, axis=0))))
    sums, gram_rows = unpack(gathered)
    gram_a = gram_rows.transpose(2, 0, 1, 3, 4).reshape(width, width)
    sums = sums.transpose(2, 1, 0, 3, 4).reshape(ny * slab, width)
    inverse, penalty = inverse_of(gram_a, gram_c)
    new_full_b = update(sums, full_b.reshape(ny * slab, width), penalty, inverse)
    new_slab_b = pick(new_full_b.reshape(ny, slab, width), y_at)
    new_b = lax.dynamic_slice_in_dim(new_slab_b, (x_at * nz + z_at) * rows_b, rows_b, 0)

    partial = contract(coords, live, blocks, slab_a, new_slab_b, 2).reshape(nx * ny, rows_c, width)
    got = lax.all_to_all(partial.astype(bf16), ("gx", "gy"), 0, 0, tiled=True)
    inverse, penalty = inverse_of(gram_a, gram_call(new_full_b))
    new_c = update(jnp.sum(got.astype(f32), axis=0), own_c, penalty, inverse)
    return new_a[None], new_b[None], new_c[None]


def solution(mesh):
    sizes = tuple(mesh.shape[name] for name in ("gx", "gy", "gz"))
    return jax.shard_map(
        functools.partial(on_device, sizes),
        mesh=mesh,
        in_specs=(
            P("gx", "gy", "gz", None, None, None, None),
            P("gx", "gy", "gz", None, None),
            P("gx", "gy", "gz"),
            P("gx", ("gy", "gz"), None),
            P("gy", ("gx", "gz"), None),
            P("gz", ("gx", "gy"), None),
        ),
        out_specs=(
            P("gx", ("gy", "gz"), None),
            P("gy", ("gx", "gz"), None),
            P("gz", ("gx", "gy"), None),
        ),
        check_vma=False,
    )
```

```python
import functools

import jax
import jax.numpy as jnp
from jax import lax
from jax.experimental import pallas as pl
from jax.experimental.pallas import tpu as pltpu
from jax.sharding import PartitionSpec as P

NS_STEPS = 8
ADMM_ITERS = 4

f32 = jnp.float32
bf16 = jnp.bfloat16

HBM = pl.BlockSpec(memory_space=pltpu.HBM)
VM = pl.BlockSpec(memory_space=pltpu.VMEM)
SM = pl.BlockSpec(memory_space=pltpu.SMEM)

SMALL = pltpu.CompilerParams(vmem_limit_bytes=12 * 2**20)
LARGE = pltpu.CompilerParams(vmem_limit_bytes=53 * 2**20)


def split(value):
    high = value.astype(bf16)
    return high, (value - high.astype(f32)).astype(bf16)


def dot3(left, right):
    left_high, left_low = split(left)
    right_high, right_low = split(right)
    mul = functools.partial(jnp.dot, preferred_element_type=f32)
    return mul(left_high, right_high) + (mul(left_low, right_high) + mul(left_high, right_low))


def gram_of(rows):
    return lax.dot_general(rows, rows, (((0,), (0,)), ((), ())), preferred_element_type=f32)


def newton_inverse(weighted):
    width = weighted.shape[0]
    row = lax.broadcasted_iota(jnp.int32, weighted.shape, 0)
    col = lax.broadcasted_iota(jnp.int32, weighted.shape, 1)
    identity = (row == col).astype(f32)
    penalty = jnp.sum(weighted * identity) / width
    system = weighted + penalty * identity
    bound = jnp.max(jnp.sum(jnp.abs(system), axis=1))
    scaled = system / bound
    product = 2.0 * identity - scaled
    scaled = 2.0 * scaled - dot3(scaled, scaled)
    for _ in range(NS_STEPS - 2):
        both = dot3(jnp.concatenate([scaled, product], axis=0), scaled)
        scaled = 2.0 * scaled - both[:width]
        product = 2.0 * product - both[width:]
    product = 2.0 * product - dot3(product, scaled)
    return penalty, product / bound


def row_update(sums, start, penalty, inverse):
    primal = start.astype(f32)
    dual = jnp.zeros_like(primal)
    for _ in range(ADMM_ITERS):
        target = dot3(sums + penalty * (primal + dual), inverse)
        primal = jnp.maximum(target - dual, 0.0)
        dual = dual + primal - target
    return primal.astype(bf16)


def contract_body(chunk, group, out_axis, coords, live, x_hbm, left_ref, right_ref, *refs):
    out_ref, (x_ref, sem, acc_ref, band_ref) = refs[0], refs[-4:]
    slots, side = x_ref.shape[0], x_ref.shape[1]
    sums_ref = refs[-5] if out_axis == 2 else out_ref

    def copy(slot, at):
        span = pl.ds(at, chunk)
        return pltpu.make_async_copy(x_hbm.at[slot, span], x_ref.at[slot, span], sem.at[slot, at // chunk])

    def start_copies(slot, _):
        for at in range(0, side, chunk):
            copy(slot, at).start()
        return 0

    def visit(slot, _):
        start = [pl.multiple_of(coords[3 * slot + mode] * side, side) for mode in range(3)]
        if out_axis == 0:
            right = right_ref[pl.ds(start[2], side), :]
            band_ref[...] = left_ref[pl.ds(start[1], side), :].astype(f32)
        else:
            right = right_ref[pl.ds(start[3 - out_axis], side), :]
            band_ref[...] = left_ref[pl.ds(start[0], side), :].astype(f32)
            acc_ref[...] = jnp.zeros_like(acc_ref)
        for at in range(0, side, group):
            if at % chunk == 0:
                copy(slot, at).wait()
            block = x_ref[slot, at : at + group]
            if out_axis == 2:
                block = jnp.swapaxes(block, 1, 2)
            terms = jnp.dot(block.reshape(group * side, side), right, preferred_element_type=f32)
            terms = terms.reshape(group, side, -1)
            if out_axis == 0:
                acc_ref[at : at + group, :] = jnp.sum(terms * band_ref[...][None], axis=1)
            else:
                acc_ref[...] += jnp.sum(terms * band_ref[at : at + group, :][:, None, :], axis=0)
        sums_ref[pl.ds(start[out_axis], side), :] += acc_ref[...]
        return 0

    total = jnp.minimum(live[0], slots)
    lax.fori_loop(0, total, start_copies, 0)
    sums_ref[...] = jnp.zeros_like(sums_ref)
    if out_axis == 1:
        refs[1][...] = gram_of(left_ref[...])
    lax.fori_loop(0, total, visit, 0)
    if out_axis == 2:
        out_ref[...] = sums_ref[...].astype(out_ref.dtype)


def contract(coords, live, blocks, left, right, out_axis):
    slots, side = blocks.shape[0], blocks.shape[1]
    chunk = group = min(32, side)
    height, width = left.shape
    outs = [jax.ShapeDtypeStruct((height, width), bf16 if out_axis == 2 else f32)]
    scratch = [
        pltpu.VMEM(blocks.shape, blocks.dtype),
        pltpu.SemaphoreType.DMA((slots, side // chunk)),
        pltpu.VMEM((side, width), f32),
        pltpu.VMEM((side, width), f32),
    ]
    if out_axis == 1:
        outs.append(jax.ShapeDtypeStruct((width, width), f32))
    if out_axis == 2:
        scratch = [pltpu.VMEM((height, width), f32)] + scratch
    return pl.pallas_call(
        functools.partial(contract_body, chunk, group, out_axis),
        in_specs=[SM, SM, HBM, VM, VM],
        out_specs=[VM] * len(outs),
        out_shape=outs,
        scratch_shapes=scratch,
        name=f"contract_{out_axis}",
        compiler_params=LARGE,
    )(coords, live, blocks, left, right)


def first_inverse_body(b_ref, c_ref, gram_c_ref, inverse_ref, penalty_ref):
    gram_c = gram_of(c_ref[...])
    gram_c_ref[...] = gram_c
    penalty_ref[0, 0], inverse_ref[...] = newton_inverse(gram_of(b_ref[...]) * gram_c)


def first_inverse(rows_b, rows_c):
    square = jax.ShapeDtypeStruct((rows_b.shape[1],) * 2, f32)
    return pl.pallas_call(
        first_inverse_body,
        out_shape=(square, square, jax.ShapeDtypeStruct((1, 1), f32)),
        out_specs=(VM, VM, SM),
        name="first_inverse",
        compiler_params=SMALL,
    )(rows_b, rows_c)


def inverse_body(left_ref, right_ref, inverse_ref, penalty_ref):
    penalty_ref[0, 0], inverse_ref[...] = newton_inverse(left_ref[...] * right_ref[...])


def inverse_of(gram_left, gram_right):
    return pl.pallas_call(
        inverse_body,
        out_shape=(jax.ShapeDtypeStruct(gram_left.shape, f32), jax.ShapeDtypeStruct((1, 1), f32)),
        out_specs=(VM, SM),
        name="inverse",
        compiler_params=SMALL,
    )(gram_left, gram_right)


def update_body(sums_ref, start_ref, penalty_ref, inverse_ref, out_ref):
    out_ref[...] = row_update(sums_ref[...], start_ref[...], penalty_ref[0, 0], inverse_ref[...])


def update(sums, start, penalty, inverse):
    return pl.pallas_call(
        update_body,
        in_specs=[VM, VM, SM, VM],
        out_shape=jax.ShapeDtypeStruct(start.shape, bf16),
        out_specs=VM,
        name="update",
        compiler_params=SMALL,
    )(sums, start, penalty, inverse)


def second_update_body(left_ref, right_ref, sums_ref, start_ref, out_ref):
    penalty, inverse = newton_inverse(left_ref[...] * right_ref[...])
    out_ref[...] = row_update(sums_ref[...], start_ref[...], penalty, inverse)


def second_update(gram_left, gram_right, sums, start):
    return pl.pallas_call(
        second_update_body,
        out_shape=jax.ShapeDtypeStruct(start.shape, bf16),
        out_specs=VM,
        name="second_update",
        compiler_params=SMALL,
    )(gram_left, gram_right, sums, start)


def gram_body(rows_ref, out_ref):
    out_ref[...] = gram_of(rows_ref[...])


def gram_call(rows):
    return pl.pallas_call(
        gram_body,
        out_shape=jax.ShapeDtypeStruct((rows.shape[1],) * 2, f32),
        out_specs=VM,
        name="gram",
        compiler_params=SMALL,
    )(rows)


def on_device(sizes, tensor_blocks, block_coords, live_counts, factor_a, factor_b, factor_c):
    nx, ny, nz = sizes
    x_at, y_at, z_at = (lax.axis_index(name) for name in ("gx", "gy", "gz"))
    slot_count, side = tensor_blocks.shape[3], tensor_blocks.shape[4]
    width = factor_a.shape[2]
    blocks = tensor_blocks.reshape(slot_count, side, side, side)
    coords = block_coords.reshape(slot_count * 3)
    live = live_counts.reshape(1)
    own_a, own_b, own_c = factor_a[0], factor_b[0], factor_c[0]
    rows_a, rows_b, rows_c = own_a.shape[0], own_b.shape[0], own_c.shape[0]
    slab = rows_a * ny * nz

    def pick(array, at, axis=0):
        return lax.dynamic_index_in_dim(array, at, axis, keepdims=False)

    def swap_cores(value):
        return lax.ppermute(value, "gz", [(0, 1), (1, 0)])

    def both_cores(value):
        other = swap_cores(value)
        return jnp.where(z_at == 0, jnp.stack([value, other]), jnp.stack([other, value]))

    def spread(value):
        sent = jnp.broadcast_to(value[None], (nx * ny,) + value.shape)
        got = lax.all_to_all(sent, ("gx", "gy"), 0, 0, tiled=True)
        return got.reshape((nx, ny) + value.shape)

    gathered = both_cores(spread(jnp.concatenate([own_b, own_c], axis=0)))
    full_b = gathered[:, :, :, :rows_b].transpose(2, 1, 0, 3, 4).reshape(ny, slab, width)
    full_c = gathered[:, :, :, rows_b:].reshape(nz, slab, width)
    slab_b, slab_c = pick(full_b, y_at), pick(full_c, z_at)

    (partial,) = contract(coords, live, blocks, slab_b, slab_c, 0)
    partial = partial.reshape(ny, nz, rows_a, width)
    sums = pick(partial, z_at, 1) + swap_cores(pick(partial, 1 - z_at, 1))
    sums = sums.reshape(ny * rows_a, width)
    gram_c, inverse, penalty = first_inverse(full_b.reshape(ny * slab, width), full_c.reshape(nz * slab, width))
    if ny == 2:
        height = ny * rows_a
        high = lax.reduce_precision(sums, 8, 7)
        sent = jnp.concatenate([high.astype(bf16), (sums - high).astype(bf16), own_a], axis=0)
        got = lax.ppermute(sent, "gy", [(0, 1), (1, 0)])
        sums = (sent[:height].astype(f32) + sent[height : 2 * height].astype(f32)) + (
            got[:height].astype(f32) + got[height : 2 * height].astype(f32)
        )
        other_a = got[2 * height :]
        start_a = jnp.where(y_at == 0, jnp.concatenate([own_a, other_a]), jnp.concatenate([other_a, own_a]))
    else:
        sums = lax.psum(sums, "gy")
        start_a = lax.all_gather(own_a, "gy", axis=0, tiled=True)
    half_a = update(sums, start_a, penalty, inverse)
    slab_a = both_cores(half_a.reshape(ny, rows_a, width)).transpose(1, 0, 2, 3).reshape(slab, width)
    new_a = pick(half_a.reshape(ny, rows_a, width), y_at)

    partial, gram = contract(coords, live, blocks, slab_a, slab_c, 1)
    partial = partial.reshape(nx, nz, rows_b, width)
    share = width // nz
    rows_g = share // nx
    gram_part = lax.dynamic_slice_in_dim(gram, z_at * share, share, 0)
    sums = pick(partial, z_at, 1) + swap_cores(pick(partial, 1 - z_at, 1))

    def pack(sums_rows, gram_rows):
        return jnp.concatenate([sums_rows, gram_rows], axis=-2)

    def unpack(packed):
        return packed[..., :rows_b, :], packed[..., rows_b:, :]

    got = lax.all_to_all(pack(sums, gram_part.reshape(nx, rows_g, width)), "gx", 0, 0, tiled=True)
    sent = jnp.broadcast_to(jnp.sum(got, axis=0)[None], got.shape)
    gathered = both_cores(lax.all_to_all(sent, "gx", 0, 0, tiled=True))
    sums, gram_rows = unpack(gathered)
    gram_a = gram_rows.reshape(width, width)
    sums = sums.transpose(1, 0, 2, 3).reshape(slab, width)
    new_slab_b = second_update(gram_a, gram_c, sums, slab_b)
    new_b = lax.dynamic_slice_in_dim(new_slab_b, (x_at * nz + z_at) * rows_b, rows_b, 0)
    if ny == 2:
        other_b = lax.ppermute(new_slab_b, "gy", [(0, 1), (1, 0)])
        gram_b_new = gram_call(jnp.concatenate([new_slab_b, other_b]))
    else:
        gram_b_new = gram_call(lax.all_gather(new_slab_b, "gy", axis=0, tiled=True))

    (partial,) = contract(coords, live, blocks, slab_a, new_slab_b, 2)
    got = lax.all_to_all(partial.reshape(nx * ny, rows_c, width), ("gx", "gy"), 0, 0, tiled=True)
    inverse, penalty = inverse_of(gram_a, gram_b_new)
    new_c = update(jnp.sum(got.astype(f32), axis=0), own_c, penalty, inverse)
    return new_a[None], new_b[None], new_c[None]


def solution(mesh):
    sizes = tuple(mesh.shape[name] for name in ("gx", "gy", "gz"))
    return jax.shard_map(
        functools.partial(on_device, sizes),
        mesh=mesh,
        in_specs=(
            P("gx", "gy", "gz", None, None, None, None),
            P("gx", "gy", "gz", None, None),
            P("gx", "gy", "gz"),
            P("gx", ("gy", "gz"), None),
            P("gy", ("gx", "gz"), None),
            P("gz", ("gx", "gy"), None),
        ),
        out_specs=(
            P("gx", ("gy", "gz"), None),
            P("gy", ("gx", "gz"), None),
            P("gz", ("gx", "gy"), None),
        ),
        check_vma=False,
    )
```

```python
import functools

import jax
import jax.numpy as jnp
from jax import lax
from jax.experimental import pallas as pl
from jax.experimental.pallas import tpu as pltpu
from jax.sharding import PartitionSpec as P

NS_STEPS = 8
ADMM_ITERS = 4

f32 = jnp.float32
bf16 = jnp.bfloat16

HBM = pl.BlockSpec(memory_space=pltpu.HBM)
VM = pl.BlockSpec(memory_space=pltpu.VMEM)
SM = pl.BlockSpec(memory_space=pltpu.SMEM)

SMALL = pltpu.CompilerParams(vmem_limit_bytes=12 * 2**20)
LARGE = pltpu.CompilerParams(vmem_limit_bytes=53 * 2**20)


def split(value):
    high = value.astype(bf16)
    return high, (value - high.astype(f32)).astype(bf16)


def dot3(left, right):
    left_high, left_low = split(left)
    right_high, right_low = split(right)
    mul = functools.partial(jnp.dot, preferred_element_type=f32)
    return mul(left_high, right_high) + (mul(left_low, right_high) + mul(left_high, right_low))


def gram_of(rows):
    return lax.dot_general(rows, rows, (((0,), (0,)), ((), ())), preferred_element_type=f32)


def newton_inverse(weighted):
    width = weighted.shape[0]
    row = lax.broadcasted_iota(jnp.int32, weighted.shape, 0)
    col = lax.broadcasted_iota(jnp.int32, weighted.shape, 1)
    identity = (row == col).astype(f32)
    penalty = jnp.sum(weighted * identity) / width
    system = weighted + penalty * identity
    bound = jnp.max(jnp.sum(jnp.abs(system), axis=1))
    scaled = system / bound
    product = 2.0 * identity - scaled
    scaled = 2.0 * scaled - dot3(scaled, scaled)
    for _ in range(NS_STEPS - 2):
        both = dot3(jnp.concatenate([scaled, product], axis=0), scaled)
        scaled = 2.0 * scaled - both[:width]
        product = 2.0 * product - both[width:]
    product = 2.0 * product - dot3(product, scaled)
    return penalty, product / bound


def row_update(sums, start, penalty, inverse):
    primal = start.astype(f32)
    dual = jnp.zeros_like(primal)
    for _ in range(ADMM_ITERS):
        target = dot3(sums + penalty * (primal + dual), inverse)
        primal = jnp.maximum(target - dual, 0.0)
        dual = dual + primal - target
    return primal.astype(bf16)


def contract_body(chunks, group, out_axis, coords, live, x_hbm, left_ref, right_ref, *refs):
    out_ref, (x_ref, sem, acc_ref, band_ref) = refs[0], refs[-4:]
    slots, side = x_ref.shape[0], x_ref.shape[1]
    sums_ref = refs[-5] if out_axis == 2 else out_ref

    def copy(slot, n):
        span = pl.ds(*chunks[n])
        return pltpu.make_async_copy(x_hbm.at[slot, span], x_ref.at[slot, span], sem.at[slot, n])

    def start_copies(slot, _):
        for n in range(len(chunks)):
            copy(slot, n).start()
        return 0

    def visit(slot, _):
        start = [pl.multiple_of(coords[3 * slot + mode] * side, side) for mode in range(3)]
        if out_axis == 0:
            right = right_ref[pl.ds(start[2], side), :]
            band_ref[...] = left_ref[pl.ds(start[1], side), :].astype(f32)
        else:
            right = right_ref[pl.ds(start[3 - out_axis], side), :]
            band_ref[...] = left_ref[pl.ds(start[0], side), :].astype(f32)
            acc_ref[...] = jnp.zeros_like(acc_ref)
        for at in range(0, side, group):
            for n in range(len(chunks)):
                if chunks[n][0] == at:
                    copy(slot, n).wait()
            block = x_ref[slot, at : at + group]
            if out_axis == 2:
                block = jnp.swapaxes(block, 1, 2)
            terms = jnp.dot(block.reshape(group * side, side), right, preferred_element_type=f32)
            terms = terms.reshape(group, side, -1)
            if out_axis == 0:
                acc_ref[at : at + group, :] = jnp.sum(terms * band_ref[...][None], axis=1)
            else:
                acc_ref[...] += jnp.sum(terms * band_ref[at : at + group, :][:, None, :], axis=0)
        sums_ref[pl.ds(start[out_axis], side), :] += acc_ref[...]
        return 0

    total = jnp.minimum(live[0], slots)
    lax.fori_loop(0, total, start_copies, 0)
    sums_ref[...] = jnp.zeros_like(sums_ref)
    if out_axis == 1:
        refs[1][...] = gram_of(left_ref[...])
    lax.fori_loop(0, total, visit, 0)
    if out_axis == 2:
        out_ref[...] = sums_ref[...].astype(out_ref.dtype)


def contract(coords, live, blocks, left, right, out_axis):
    slots, side = blocks.shape[0], blocks.shape[1]
    group = min(8, side)
    first = side // 4 // group * group or side
    chunks = [(at, size) for at, size in ((0, first), (first, side - first)) if size]
    height, width = left.shape
    outs = [jax.ShapeDtypeStruct((height, width), bf16 if out_axis == 2 else f32)]
    scratch = [
        pltpu.VMEM(blocks.shape, blocks.dtype),
        pltpu.SemaphoreType.DMA((slots, len(chunks))),
        pltpu.VMEM((side, width), f32),
        pltpu.VMEM((side, width), f32),
    ]
    if out_axis == 1:
        outs.append(jax.ShapeDtypeStruct((width, width), f32))
    if out_axis == 2:
        scratch = [pltpu.VMEM((height, width), f32)] + scratch
    return pl.pallas_call(
        functools.partial(contract_body, chunks, group, out_axis),
        in_specs=[SM, SM, HBM, VM, VM],
        out_specs=[VM] * len(outs),
        out_shape=outs,
        scratch_shapes=scratch,
        name=f"contract_{out_axis}",
        compiler_params=LARGE,
    )(coords, live, blocks, left, right)


def first_inverse_body(b_ref, c_ref, gram_c_ref, inverse_ref, penalty_ref):
    gram_c = gram_of(c_ref[...])
    gram_c_ref[...] = gram_c
    penalty_ref[0, 0], inverse_ref[...] = newton_inverse(gram_of(b_ref[...]) * gram_c)


def first_inverse(rows_b, rows_c):
    square = jax.ShapeDtypeStruct((rows_b.shape[1],) * 2, f32)
    return pl.pallas_call(
        first_inverse_body,
        out_shape=(square, square, jax.ShapeDtypeStruct((1, 1), f32)),
        out_specs=(VM, VM, SM),
        name="first_inverse",
        compiler_params=SMALL,
    )(rows_b, rows_c)


def inverse_body(left_ref, right_ref, inverse_ref, penalty_ref):
    penalty_ref[0, 0], inverse_ref[...] = newton_inverse(left_ref[...] * right_ref[...])


def inverse_of(gram_left, gram_right):
    return pl.pallas_call(
        inverse_body,
        out_shape=(jax.ShapeDtypeStruct(gram_left.shape, f32), jax.ShapeDtypeStruct((1, 1), f32)),
        out_specs=(VM, SM),
        name="inverse",
        compiler_params=SMALL,
    )(gram_left, gram_right)


def update_body(sums_ref, start_ref, penalty_ref, inverse_ref, out_ref):
    out_ref[...] = row_update(sums_ref[...], start_ref[...], penalty_ref[0, 0], inverse_ref[...])


def update(sums, start, penalty, inverse):
    return pl.pallas_call(
        update_body,
        in_specs=[VM, VM, SM, VM],
        out_shape=jax.ShapeDtypeStruct(start.shape, bf16),
        out_specs=VM,
        name="update",
        compiler_params=SMALL,
    )(sums, start, penalty, inverse)


def second_update_body(left_ref, right_ref, sums_ref, start_ref, out_ref):
    penalty, inverse = newton_inverse(left_ref[...] * right_ref[...])
    out_ref[...] = row_update(sums_ref[...], start_ref[...], penalty, inverse)


def second_update(gram_left, gram_right, sums, start):
    return pl.pallas_call(
        second_update_body,
        out_shape=jax.ShapeDtypeStruct(start.shape, bf16),
        out_specs=VM,
        name="second_update",
        compiler_params=SMALL,
    )(gram_left, gram_right, sums, start)


def gram_body(rows_ref, out_ref):
    out_ref[...] = gram_of(rows_ref[...])


def gram_call(rows):
    return pl.pallas_call(
        gram_body,
        out_shape=jax.ShapeDtypeStruct((rows.shape[1],) * 2, f32),
        out_specs=VM,
        name="gram",
        compiler_params=SMALL,
    )(rows)


def on_device(sizes, tensor_blocks, block_coords, live_counts, factor_a, factor_b, factor_c):
    nx, ny, nz = sizes
    x_at, y_at, z_at = (lax.axis_index(name) for name in ("gx", "gy", "gz"))
    slot_count, side = tensor_blocks.shape[3], tensor_blocks.shape[4]
    width = factor_a.shape[2]
    blocks = tensor_blocks.reshape(slot_count, side, side, side)
    coords = block_coords.reshape(slot_count * 3)
    live = live_counts.reshape(1)
    own_a, own_b, own_c = factor_a[0], factor_b[0], factor_c[0]
    rows_a, rows_b, rows_c = own_a.shape[0], own_b.shape[0], own_c.shape[0]
    slab = rows_a * ny * nz

    def pick(array, at, axis=0):
        return lax.dynamic_index_in_dim(array, at, axis, keepdims=False)

    def swap_cores(value):
        return lax.ppermute(value, "gz", [(0, 1), (1, 0)])

    def both_cores(value):
        other = swap_cores(value)
        return jnp.where(z_at == 0, jnp.stack([value, other]), jnp.stack([other, value]))

    def spread(value):
        sent = jnp.broadcast_to(value[None], (nx * ny,) + value.shape)
        got = lax.all_to_all(sent, ("gx", "gy"), 0, 0, tiled=True)
        return got.reshape((nx, ny) + value.shape)

    gathered = both_cores(spread(jnp.concatenate([own_b, own_c], axis=0)))
    full_b = gathered[:, :, :, :rows_b].transpose(2, 1, 0, 3, 4).reshape(ny, slab, width)
    full_c = gathered[:, :, :, rows_b:].reshape(nz, slab, width)
    slab_b, slab_c = pick(full_b, y_at), pick(full_c, z_at)

    (partial,) = contract(coords, live, blocks, slab_b, slab_c, 0)
    partial = partial.reshape(ny, nz, rows_a, width)
    sums = pick(partial, z_at, 1) + swap_cores(pick(partial, 1 - z_at, 1))
    sums = sums.reshape(ny * rows_a, width)
    gram_c, inverse, penalty = first_inverse(full_b.reshape(ny * slab, width), full_c.reshape(nz * slab, width))
    if ny == 2:
        height = ny * rows_a
        high = lax.reduce_precision(sums, 8, 7)
        sent = jnp.concatenate([high.astype(bf16), (sums - high).astype(bf16), own_a], axis=0)
        got = lax.ppermute(sent, "gy", [(0, 1), (1, 0)])
        sums = (sent[:height].astype(f32) + sent[height : 2 * height].astype(f32)) + (
            got[:height].astype(f32) + got[height : 2 * height].astype(f32)
        )
        other_a = got[2 * height :]
        start_a = jnp.where(y_at == 0, jnp.concatenate([own_a, other_a]), jnp.concatenate([other_a, own_a]))
    else:
        sums = lax.psum(sums, "gy")
        start_a = lax.all_gather(own_a, "gy", axis=0, tiled=True)
    half_a = update(sums, start_a, penalty, inverse)
    slab_a = both_cores(half_a.reshape(ny, rows_a, width)).transpose(1, 0, 2, 3).reshape(slab, width)
    new_a = pick(half_a.reshape(ny, rows_a, width), y_at)

    partial, gram = contract(coords, live, blocks, slab_a, slab_c, 1)
    partial = partial.reshape(nx, nz, rows_b, width)
    share = width // nz
    rows_g = share // nx
    gram_part = lax.dynamic_slice_in_dim(gram, z_at * share, share, 0)
    sums = pick(partial, z_at, 1) + swap_cores(pick(partial, 1 - z_at, 1))

    def pack(sums_rows, gram_rows):
        return jnp.concatenate([sums_rows, gram_rows], axis=-2)

    def unpack(packed):
        return packed[..., :rows_b, :], packed[..., rows_b:, :]

    got = lax.all_to_all(pack(sums, gram_part.reshape(nx, rows_g, width)), "gx", 0, 0, tiled=True)
    sent = jnp.broadcast_to(jnp.sum(got, axis=0)[None], got.shape)
    gathered = both_cores(lax.all_to_all(sent, "gx", 0, 0, tiled=True))
    sums, gram_rows = unpack(gathered)
    gram_a = gram_rows.reshape(width, width)
    sums = sums.transpose(1, 0, 2, 3).reshape(slab, width)
    new_slab_b = second_update(gram_a, gram_c, sums, slab_b)
    new_b = lax.dynamic_slice_in_dim(new_slab_b, (x_at * nz + z_at) * rows_b, rows_b, 0)
    if ny == 2:
        other_b = lax.ppermute(new_slab_b, "gy", [(0, 1), (1, 0)])
        gram_b_new = gram_call(jnp.concatenate([new_slab_b, other_b]))
    else:
        gram_b_new = gram_call(lax.all_gather(new_slab_b, "gy", axis=0, tiled=True))

    (partial,) = contract(coords, live, blocks, slab_a, new_slab_b, 2)
    got = lax.all_to_all(partial.reshape(nx * ny, rows_c, width), ("gx", "gy"), 0, 0, tiled=True)
    inverse, penalty = inverse_of(gram_a, gram_b_new)
    new_c = update(jnp.sum(got.astype(f32), axis=0), own_c, penalty, inverse)
    return new_a[None], new_b[None], new_c[None]


def solution(mesh):
    sizes = tuple(mesh.shape[name] for name in ("gx", "gy", "gz"))
    return jax.shard_map(
        functools.partial(on_device, sizes),
        mesh=mesh,
        in_specs=(
            P("gx", "gy", "gz", None, None, None, None),
            P("gx", "gy", "gz", None, None),
            P("gx", "gy", "gz"),
            P("gx", ("gy", "gz"), None),
            P("gy", ("gx", "gz"), None),
            P("gz", ("gx", "gy"), None),
        ),
        out_specs=(
            P("gx", ("gy", "gz"), None),
            P("gy", ("gx", "gz"), None),
            P("gz", ("gx", "gy"), None),
        ),
        check_vma=False,
    )
```

```python
import functools

import jax
import jax.numpy as jnp
from jax import lax
from jax.experimental import pallas as pl
from jax.experimental.pallas import tpu as pltpu
from jax.sharding import PartitionSpec as P

NS_STEPS = 8
ADMM_ITERS = 4

f32 = jnp.float32
bf16 = jnp.bfloat16

HBM = pl.BlockSpec(memory_space=pltpu.HBM)
VM = pl.BlockSpec(memory_space=pltpu.VMEM)
SM = pl.BlockSpec(memory_space=pltpu.SMEM)

SMALL = pltpu.CompilerParams(vmem_limit_bytes=12 * 2**20)
LARGE = pltpu.CompilerParams(vmem_limit_bytes=53 * 2**20)
FIRST = pltpu.CompilerParams(vmem_limit_bytes=37 * 2**20)
SECOND = pltpu.CompilerParams(vmem_limit_bytes=12 * 2**20)


def split(value):
    high = value.astype(bf16)
    return high, (value - high.astype(f32)).astype(bf16)


def dot3(left, right):
    left_high, left_low = split(left)
    right_high, right_low = split(right)
    mul = functools.partial(jnp.dot, preferred_element_type=f32)
    return mul(left_high, right_high) + (mul(left_low, right_high) + mul(left_high, right_low))


def gram_of(rows):
    return lax.dot_general(rows, rows, (((0,), (0,)), ((), ())), preferred_element_type=f32)


def newton_inverse(weighted):
    width = weighted.shape[0]
    row = lax.broadcasted_iota(jnp.int32, weighted.shape, 0)
    col = lax.broadcasted_iota(jnp.int32, weighted.shape, 1)
    identity = (row == col).astype(f32)
    penalty = jnp.sum(weighted * identity) / width
    system = weighted + penalty * identity
    bound = jnp.max(jnp.sum(jnp.abs(system), axis=1))
    scaled = system / bound
    product = 2.0 * identity - scaled
    scaled = 2.0 * scaled - dot3(scaled, scaled)
    for _ in range(NS_STEPS - 2):
        both = dot3(jnp.concatenate([scaled, product], axis=0), scaled)
        scaled = 2.0 * scaled - both[:width]
        product = 2.0 * product - both[width:]
    product = 2.0 * product - dot3(product, scaled)
    return penalty, product / bound


def row_update(sums, start, penalty, inverse):
    primal = start.astype(f32)
    dual = jnp.zeros_like(primal)
    for _ in range(ADMM_ITERS):
        target = dot3(sums + penalty * (primal + dual), inverse)
        primal = jnp.maximum(target - dual, 0.0)
        dual = dual + primal - target
    return primal.astype(bf16)


def contract_body(chunks, group, out_axis, coords, live, x_hbm, left_ref, right_ref, *refs):
    out_ref, (x_ref, sem, acc_ref, band_ref) = refs[0], refs[-4:]
    slots, side = x_ref.shape[0], x_ref.shape[1]
    sums_ref = refs[-5] if out_axis == 2 else out_ref

    def copy(slot, n):
        span = pl.ds(*chunks[n])
        return pltpu.make_async_copy(x_hbm.at[slot, span], x_ref.at[slot, span], sem.at[slot, n])

    def start_copies(slot, _):
        for n in range(len(chunks)):
            copy(slot, n).start()
        return 0

    def visit(slot, _):
        start = [pl.multiple_of(coords[3 * slot + mode] * side, side) for mode in range(3)]
        if out_axis == 0:
            right = right_ref[pl.ds(start[2], side), :]
            band_ref[...] = left_ref[pl.ds(start[1], side), :].astype(f32)
        else:
            right = right_ref[pl.ds(start[3 - out_axis], side), :]
            band_ref[...] = left_ref[pl.ds(start[0], side), :].astype(f32)
            acc_ref[...] = jnp.zeros_like(acc_ref)
        for at in range(0, side, group):
            for n in range(len(chunks)):
                if chunks[n][0] == at:
                    copy(slot, n).wait()
            block = x_ref[slot, at : at + group]
            if out_axis == 2:
                block = jnp.swapaxes(block, 1, 2)
            terms = jnp.dot(block.reshape(group * side, side), right, preferred_element_type=f32)
            terms = terms.reshape(group, side, -1)
            if out_axis == 0:

                @pl.when(slot == 0)
                def _():
                    refs[1][at : at + group] = terms

                acc_ref[at : at + group, :] = jnp.sum(terms * band_ref[...][None], axis=1)
            else:
                acc_ref[...] += jnp.sum(terms * band_ref[at : at + group, :][:, None, :], axis=0)
        sums_ref[pl.ds(start[out_axis], side), :] += acc_ref[...]
        return 0

    total = jnp.minimum(live[0], slots)
    lax.fori_loop(0, total, start_copies, 0)
    sums_ref[...] = jnp.zeros_like(sums_ref)
    lax.fori_loop(0, total, visit, 0)
    if out_axis == 2:
        out_ref[...] = sums_ref[...].astype(out_ref.dtype)


def contract(coords, live, blocks, left, right, out_axis):
    slots, side = blocks.shape[0], blocks.shape[1]
    group = min(8, side)
    first = side // 4 // group * group or side
    chunks = [(at, size) for at, size in ((0, first), (first, side - first)) if size]
    height, width = left.shape
    outs = [jax.ShapeDtypeStruct((height, width), bf16 if out_axis == 2 else f32)]
    if out_axis == 0:
        outs.append(pltpu.VMEM((side, side, width), f32))
    scratch = [
        pltpu.VMEM(blocks.shape, blocks.dtype),
        pltpu.SemaphoreType.DMA((slots, len(chunks))),
        pltpu.VMEM((side, width), f32),
        pltpu.VMEM((side, width), f32),
    ]
    if out_axis == 2:
        scratch = [pltpu.VMEM((height, width), f32)] + scratch
    return pl.pallas_call(
        functools.partial(contract_body, chunks, group, out_axis),
        in_specs=[SM, SM, HBM, VM, VM],
        out_specs=[VM] * len(outs),
        out_shape=outs,
        scratch_shapes=scratch,
        name=f"contract_{out_axis}",
        compiler_params=FIRST if out_axis == 0 else LARGE,
    )(coords, live, blocks, left, right)


def second_body(group, coords, live, x_hbm, terms_ref, left_ref, right_ref, out_ref, gram_ref, x_ref, sem, accs_ref, bands_ref):
    side = x_hbm.shape[1]
    total = jnp.minimum(live[0], x_hbm.shape[0])

    def copy(slot):
        return pltpu.make_async_copy(x_hbm.at[slot], x_ref.at[slot - 1], sem.at[slot - 1])

    def start_copy(slot, _):
        copy(slot).start()
        return 0

    lax.fori_loop(1, total, start_copy, 0)
    gram_ref[...] = gram_of(left_ref[...])
    out_ref[...] = jnp.zeros_like(out_ref)

    def open_slot(slot, place):
        start = [pl.multiple_of(coords[3 * slot + mode] * side, side) for mode in range(3)]
        bands_ref[place] = left_ref[pl.ds(start[0], side), :].astype(f32)
        accs_ref[place] = jnp.zeros(accs_ref.shape[1:], f32)
        return start

    def add_kept(at):
        weights = bands_ref[0, at : at + group, :][:, None, :]
        accs_ref[0] += jnp.sum(terms_ref[at : at + group] * weights, axis=0)

    def visit(slot, with_kept):
        start = open_slot(slot, 1)
        right = right_ref[pl.ds(start[2], side), :]
        copy(slot).wait()
        for at in range(0, side, group):
            block = x_ref[slot - 1, at : at + group].reshape(group * side, side)
            terms = jnp.dot(block, right, preferred_element_type=f32).reshape(group, side, -1)
            if with_kept:
                add_kept(at)
            accs_ref[1] += jnp.sum(terms * bands_ref[1, at : at + group, :][:, None, :], axis=0)
        out_ref[pl.ds(start[1], side), :] += accs_ref[1]
        return 0

    first = open_slot(0, 0)

    @pl.when(total == 1)
    def _():
        for at in range(0, side, group):
            add_kept(at)

    @pl.when(total > 1)
    def _():
        visit(1, True)

    out_ref[pl.ds(first[1], side), :] += accs_ref[0]
    lax.fori_loop(2, total, lambda slot, _: visit(slot, False), 0)


def second_contract(coords, live, blocks, terms, left, right):
    slots, side = blocks.shape[0], blocks.shape[1]
    height, width = left.shape
    others = max(slots - 1, 1)
    return pl.pallas_call(
        functools.partial(second_body, min(8, side)),
        in_specs=[SM, SM, HBM, VM, VM, VM],
        out_specs=[VM, VM],
        out_shape=[jax.ShapeDtypeStruct((height, width), f32), jax.ShapeDtypeStruct((width, width), f32)],
        scratch_shapes=[
            pltpu.VMEM((others,) + blocks.shape[1:], blocks.dtype),
            pltpu.SemaphoreType.DMA((others,)),
            pltpu.VMEM((2, side, width), f32),
            pltpu.VMEM((2, side, width), f32),
        ],
        name="contract_1",
        compiler_params=SECOND,
    )(coords, live, blocks, terms, left, right)


def first_inverse_body(b_ref, c_ref, gram_c_ref, inverse_ref, penalty_ref):
    gram_c = gram_of(c_ref[...])
    gram_c_ref[...] = gram_c
    penalty_ref[0, 0], inverse_ref[...] = newton_inverse(gram_of(b_ref[...]) * gram_c)


def first_inverse(rows_b, rows_c):
    square = jax.ShapeDtypeStruct((rows_b.shape[1],) * 2, f32)
    return pl.pallas_call(
        first_inverse_body,
        out_shape=(square, square, jax.ShapeDtypeStruct((1, 1), f32)),
        out_specs=(VM, VM, SM),
        name="first_inverse",
        compiler_params=SMALL,
    )(rows_b, rows_c)


def inverse_body(left_ref, right_ref, inverse_ref, penalty_ref):
    penalty_ref[0, 0], inverse_ref[...] = newton_inverse(left_ref[...] * right_ref[...])


def inverse_of(gram_left, gram_right):
    return pl.pallas_call(
        inverse_body,
        out_shape=(jax.ShapeDtypeStruct(gram_left.shape, f32), jax.ShapeDtypeStruct((1, 1), f32)),
        out_specs=(VM, SM),
        name="inverse",
        compiler_params=SMALL,
    )(gram_left, gram_right)


def update_body(sums_ref, start_ref, penalty_ref, inverse_ref, out_ref):
    out_ref[...] = row_update(sums_ref[...], start_ref[...], penalty_ref[0, 0], inverse_ref[...])


def update(sums, start, penalty, inverse):
    return pl.pallas_call(
        update_body,
        in_specs=[VM, VM, SM, VM],
        out_shape=jax.ShapeDtypeStruct(start.shape, bf16),
        out_specs=VM,
        name="update",
        compiler_params=SMALL,
    )(sums, start, penalty, inverse)


def second_update_body(left_ref, right_ref, sums_ref, start_ref, out_ref):
    penalty, inverse = newton_inverse(left_ref[...] * right_ref[...])
    out_ref[...] = row_update(sums_ref[...], start_ref[...], penalty, inverse)


def second_update(gram_left, gram_right, sums, start):
    return pl.pallas_call(
        second_update_body,
        out_shape=jax.ShapeDtypeStruct(start.shape, bf16),
        out_specs=VM,
        name="second_update",
        compiler_params=SMALL,
    )(gram_left, gram_right, sums, start)


def gram_body(rows_ref, out_ref):
    out_ref[...] = gram_of(rows_ref[...])


def gram_call(rows):
    return pl.pallas_call(
        gram_body,
        out_shape=jax.ShapeDtypeStruct((rows.shape[1],) * 2, f32),
        out_specs=VM,
        name="gram",
        compiler_params=SMALL,
    )(rows)


def on_device(sizes, tensor_blocks, block_coords, live_counts, factor_a, factor_b, factor_c):
    nx, ny, nz = sizes
    x_at, y_at, z_at = (lax.axis_index(name) for name in ("gx", "gy", "gz"))
    slot_count, side = tensor_blocks.shape[3], tensor_blocks.shape[4]
    width = factor_a.shape[2]
    blocks = tensor_blocks.reshape(slot_count, side, side, side)
    coords = block_coords.reshape(slot_count * 3)
    live = live_counts.reshape(1)
    own_a, own_b, own_c = factor_a[0], factor_b[0], factor_c[0]
    rows_a, rows_b, rows_c = own_a.shape[0], own_b.shape[0], own_c.shape[0]
    slab = rows_a * ny * nz

    def pick(array, at, axis=0):
        return lax.dynamic_index_in_dim(array, at, axis, keepdims=False)

    def swap_cores(value):
        return lax.ppermute(value, "gz", [(0, 1), (1, 0)])

    def both_cores(value):
        other = swap_cores(value)
        return jnp.where(z_at == 0, jnp.stack([value, other]), jnp.stack([other, value]))

    def spread(value):
        sent = jnp.broadcast_to(value[None], (nx * ny,) + value.shape)
        got = lax.all_to_all(sent, ("gx", "gy"), 0, 0, tiled=True)
        return got.reshape((nx, ny) + value.shape)

    gathered = both_cores(spread(jnp.concatenate([own_b, own_c], axis=0)))
    full_b = gathered[:, :, :, :rows_b].transpose(2, 1, 0, 3, 4).reshape(ny, slab, width)
    full_c = gathered[:, :, :, rows_b:].reshape(nz, slab, width)
    slab_b = jnp.where(y_at == 0, full_b[0], full_b[1]) if ny == 2 else pick(full_b, y_at)
    slab_c = pick(full_c, z_at)

    partial, terms = contract(coords, live, blocks, slab_b, slab_c, 0)
    partial = partial.reshape(ny, nz, rows_a, width)
    sums = pick(partial, z_at, 1) + swap_cores(pick(partial, 1 - z_at, 1))
    sums = sums.reshape(ny * rows_a, width)
    gram_c, inverse, penalty = first_inverse(full_b.reshape(ny * slab, width), full_c.reshape(nz * slab, width))
    if ny == 2:
        height = ny * rows_a
        high = lax.reduce_precision(sums, 8, 7)
        sent = jnp.concatenate([high.astype(bf16), (sums - high).astype(bf16), own_a], axis=0)
        got = lax.ppermute(sent, "gy", [(0, 1), (1, 0)])
        sums = (sent[:height].astype(f32) + sent[height : 2 * height].astype(f32)) + (
            got[:height].astype(f32) + got[height : 2 * height].astype(f32)
        )
        other_a = got[2 * height :]
        start_a = jnp.where(y_at == 0, jnp.concatenate([own_a, other_a]), jnp.concatenate([other_a, own_a]))
    else:
        sums = lax.psum(sums, "gy")
        start_a = lax.all_gather(own_a, "gy", axis=0, tiled=True)
    half_a = update(sums, start_a, penalty, inverse)
    slab_a = both_cores(half_a.reshape(ny, rows_a, width)).transpose(1, 0, 2, 3).reshape(slab, width)
    new_a = pick(half_a.reshape(ny, rows_a, width), y_at)

    partial, gram = second_contract(coords, live, blocks, terms, slab_a, slab_c)
    partial = partial.reshape(nx, nz, rows_b, width)
    share = width // nz
    rows_g = share // nx
    gram_part = lax.dynamic_slice_in_dim(gram, z_at * share, share, 0)
    sums = pick(partial, z_at, 1) + swap_cores(pick(partial, 1 - z_at, 1))

    def pack(sums_rows, gram_rows):
        return jnp.concatenate([sums_rows, gram_rows], axis=-2)

    def unpack(packed):
        return packed[..., :rows_b, :], packed[..., rows_b:, :]

    got = lax.all_to_all(pack(sums, gram_part.reshape(nx, rows_g, width)), "gx", 0, 0, tiled=True)
    sent = jnp.broadcast_to(jnp.sum(got, axis=0)[None], got.shape)
    gathered = both_cores(lax.all_to_all(sent, "gx", 0, 0, tiled=True))
    sums, gram_rows = unpack(gathered)
    gram_a = gram_rows.reshape(width, width)
    sums = sums.transpose(1, 0, 2, 3).reshape(slab, width)
    new_slab_b = second_update(gram_a, gram_c, sums, slab_b)
    new_b = lax.dynamic_slice_in_dim(new_slab_b, (x_at * nz + z_at) * rows_b, rows_b, 0)
    if ny == 2:
        other_b = lax.ppermute(new_slab_b, "gy", [(0, 1), (1, 0)])
        gram_b_new = gram_call(jnp.concatenate([new_slab_b, other_b]))
    else:
        gram_b_new = gram_call(lax.all_gather(new_slab_b, "gy", axis=0, tiled=True))

    (partial,) = contract(coords, live, blocks, slab_a, new_slab_b, 2)
    got = lax.all_to_all(partial.reshape(nx * ny, rows_c, width), ("gx", "gy"), 0, 0, tiled=True)
    inverse, penalty = inverse_of(gram_a, gram_b_new)
    new_c = update(jnp.sum(got.astype(f32), axis=0), own_c, penalty, inverse)
    return new_a[None], new_b[None], new_c[None]


def solution(mesh):
    sizes = tuple(mesh.shape[name] for name in ("gx", "gy", "gz"))
    return jax.shard_map(
        functools.partial(on_device, sizes),
        mesh=mesh,
        in_specs=(
            P("gx", "gy", "gz", None, None, None, None),
            P("gx", "gy", "gz", None, None),
            P("gx", "gy", "gz"),
            P("gx", ("gy", "gz"), None),
            P("gy", ("gx", "gz"), None),
            P("gz", ("gx", "gy"), None),
        ),
        out_specs=(
            P("gx", ("gy", "gz"), None),
            P("gy", ("gx", "gz"), None),
            P("gz", ("gx", "gy"), None),
        ),
        check_vma=False,
    )
```

```python
import functools

import jax
import jax.numpy as jnp
from jax import lax
from jax.experimental import pallas as pl
from jax.experimental.pallas import tpu as pltpu
from jax.sharding import PartitionSpec as P

NS_STEPS = 8
ADMM_ITERS = 4

f32 = jnp.float32
bf16 = jnp.bfloat16

HBM = pl.BlockSpec(memory_space=pltpu.HBM)
VM = pl.BlockSpec(memory_space=pltpu.VMEM)
SM = pl.BlockSpec(memory_space=pltpu.SMEM)

SMALL = pltpu.CompilerParams(vmem_limit_bytes=12 * 2**20)
LARGE = pltpu.CompilerParams(vmem_limit_bytes=53 * 2**20)
FIRST = pltpu.CompilerParams(vmem_limit_bytes=37 * 2**20)
SECOND = pltpu.CompilerParams(vmem_limit_bytes=12 * 2**20)


def split(value):
    high = value.astype(bf16)
    return high, (value - high.astype(f32)).astype(bf16)


def dot3(left, right):
    left_high, left_low = split(left)
    right_high, right_low = split(right)
    mul = functools.partial(jnp.dot, preferred_element_type=f32)
    return mul(left_high, right_high) + (mul(left_low, right_high) + mul(left_high, right_low))


def gram_of(rows):
    return lax.dot_general(rows, rows, (((0,), (0,)), ((), ())), preferred_element_type=f32)


def newton_inverse(weighted):
    width = weighted.shape[0]
    row = lax.broadcasted_iota(jnp.int32, weighted.shape, 0)
    col = lax.broadcasted_iota(jnp.int32, weighted.shape, 1)
    identity = (row == col).astype(f32)
    penalty = jnp.sum(weighted * identity) / width
    system = weighted + penalty * identity
    bound = jnp.max(jnp.sum(jnp.abs(system), axis=1))
    scaled = system / bound
    product = 2.0 * identity - scaled
    scaled = 2.0 * scaled - dot3(scaled, scaled)
    for _ in range(NS_STEPS - 2):
        both = dot3(jnp.concatenate([scaled, product], axis=0), scaled)
        scaled = 2.0 * scaled - both[:width]
        product = 2.0 * product - both[width:]
    product = 2.0 * product - dot3(product, scaled)
    return penalty, product / bound


def row_update(sums, start, penalty, inverse):
    primal = start.astype(f32)
    dual = jnp.zeros_like(primal)
    for _ in range(ADMM_ITERS):
        target = dot3(sums + penalty * (primal + dual), inverse)
        primal = jnp.maximum(target - dual, 0.0)
        dual = dual + primal - target
    return primal.astype(bf16)


def contract_body(chunks, group, out_axis, coords, live, x_hbm, left_ref, right_ref, *refs):
    out_ref, (x_ref, sem, acc_ref, band_ref) = refs[0], refs[-4:]
    slots, side = x_ref.shape[0], x_ref.shape[1]
    sums_ref = refs[-5] if out_axis == 2 else out_ref

    def copy(slot, n):
        span = pl.ds(*chunks[n])
        return pltpu.make_async_copy(x_hbm.at[slot, span], x_ref.at[slot, span], sem.at[slot, n])

    total = jnp.minimum(live[0], slots)

    def start_copies(step, _):
        for n in range(len(chunks)):
            copy(total - 1 - step, n).start()
        return 0

    def visit(step, _):
        slot = total - 1 - step
        start = [pl.multiple_of(coords[3 * slot + mode] * side, side) for mode in range(3)]
        if out_axis == 0:
            right = right_ref[pl.ds(start[2], side), :]
            band_ref[...] = left_ref[pl.ds(start[1], side), :].astype(f32)
        else:
            right = right_ref[pl.ds(start[3 - out_axis], side), :]
            band_ref[...] = left_ref[pl.ds(start[0], side), :].astype(f32)
            acc_ref[...] = jnp.zeros_like(acc_ref)
        for at in range(0, side, group):
            for n in range(len(chunks)):
                if chunks[n][0] == at:
                    copy(slot, n).wait()
            block = x_ref[slot, at : at + group]
            if out_axis == 2:
                block = jnp.swapaxes(block, 1, 2)
            terms = jnp.dot(block.reshape(group * side, side), right, preferred_element_type=f32)
            terms = terms.reshape(group, side, -1)
            if out_axis == 0:
                refs[1][at : at + group] = terms
                acc_ref[at : at + group, :] = jnp.sum(terms * band_ref[...][None], axis=1)
            else:
                acc_ref[...] += jnp.sum(terms * band_ref[at : at + group, :][:, None, :], axis=0)
        sums_ref[pl.ds(start[out_axis], side), :] += acc_ref[...]
        return 0

    lax.fori_loop(0, total, start_copies, 0)
    sums_ref[...] = jnp.zeros_like(sums_ref)
    lax.fori_loop(0, total, visit, 0)
    if out_axis == 2:
        out_ref[...] = sums_ref[...].astype(out_ref.dtype)


def contract(coords, live, blocks, left, right, out_axis):
    slots, side = blocks.shape[0], blocks.shape[1]
    group = min(8, side)
    first = side // 4 // group * group or side
    chunks = [(at, size) for at, size in ((0, first), (first, side - first)) if size]
    height, width = left.shape
    outs = [jax.ShapeDtypeStruct((height, width), bf16 if out_axis == 2 else f32)]
    if out_axis == 0:
        outs.append(pltpu.VMEM((side, side, width), f32))
    scratch = [
        pltpu.VMEM(blocks.shape, blocks.dtype),
        pltpu.SemaphoreType.DMA((slots, len(chunks))),
        pltpu.VMEM((side, width), f32),
        pltpu.VMEM((side, width), f32),
    ]
    if out_axis == 2:
        scratch = [pltpu.VMEM((height, width), f32)] + scratch
    return pl.pallas_call(
        functools.partial(contract_body, chunks, group, out_axis),
        in_specs=[SM, SM, HBM, VM, VM],
        out_specs=[VM] * len(outs),
        out_shape=outs,
        scratch_shapes=scratch,
        name=f"contract_{out_axis}",
        compiler_params=FIRST if out_axis == 0 else LARGE,
    )(coords, live, blocks, left, right)


def second_body(group, coords, live, x_hbm, terms_ref, left_ref, right_ref, out_ref, gram_ref, x_ref, sem, accs_ref, bands_ref):
    side = x_hbm.shape[1]
    total = jnp.minimum(live[0], x_hbm.shape[0])

    def copy(slot):
        return pltpu.make_async_copy(x_hbm.at[slot], x_ref.at[slot - 1], sem.at[slot - 1])

    def start_copy(slot, _):
        copy(slot).start()
        return 0

    lax.fori_loop(1, total, start_copy, 0)
    gram_ref[...] = gram_of(left_ref[...])
    out_ref[...] = jnp.zeros_like(out_ref)

    def open_slot(slot, place):
        start = [pl.multiple_of(coords[3 * slot + mode] * side, side) for mode in range(3)]
        bands_ref[place] = left_ref[pl.ds(start[0], side), :].astype(f32)
        accs_ref[place] = jnp.zeros(accs_ref.shape[1:], f32)
        return start

    def add_kept(at):
        weights = bands_ref[0, at : at + group, :][:, None, :]
        accs_ref[0] += jnp.sum(terms_ref[at : at + group] * weights, axis=0)

    def visit(slot, with_kept):
        start = open_slot(slot, 1)
        right = right_ref[pl.ds(start[2], side), :]
        copy(slot).wait()
        for at in range(0, side, group):
            block = x_ref[slot - 1, at : at + group].reshape(group * side, side)
            terms = jnp.dot(block, right, preferred_element_type=f32).reshape(group, side, -1)
            if with_kept:
                add_kept(at)
            accs_ref[1] += jnp.sum(terms * bands_ref[1, at : at + group, :][:, None, :], axis=0)
        out_ref[pl.ds(start[1], side), :] += accs_ref[1]
        return 0

    first = open_slot(0, 0)

    @pl.when(total == 1)
    def _():
        for at in range(0, side, group):
            add_kept(at)

    @pl.when(total > 1)
    def _():
        visit(1, True)

    out_ref[pl.ds(first[1], side), :] += accs_ref[0]
    lax.fori_loop(2, total, lambda slot, _: visit(slot, False), 0)


def second_contract(coords, live, blocks, terms, left, right):
    slots, side = blocks.shape[0], blocks.shape[1]
    height, width = left.shape
    others = max(slots - 1, 1)
    return pl.pallas_call(
        functools.partial(second_body, min(8, side)),
        in_specs=[SM, SM, HBM, VM, VM, VM],
        out_specs=[VM, VM],
        out_shape=[jax.ShapeDtypeStruct((height, width), f32), jax.ShapeDtypeStruct((width, width), f32)],
        scratch_shapes=[
            pltpu.VMEM((others,) + blocks.shape[1:], blocks.dtype),
            pltpu.SemaphoreType.DMA((others,)),
            pltpu.VMEM((2, side, width), f32),
            pltpu.VMEM((2, side, width), f32),
        ],
        name="contract_1",
        compiler_params=SECOND,
    )(coords, live, blocks, terms, left, right)


def first_inverse_body(b_ref, c_ref, gram_c_ref, inverse_ref, penalty_ref):
    gram_c = gram_of(c_ref[...])
    gram_c_ref[...] = gram_c
    penalty_ref[0, 0], inverse_ref[...] = newton_inverse(gram_of(b_ref[...]) * gram_c)


def first_inverse(rows_b, rows_c):
    square = jax.ShapeDtypeStruct((rows_b.shape[1],) * 2, f32)
    return pl.pallas_call(
        first_inverse_body,
        out_shape=(square, square, jax.ShapeDtypeStruct((1, 1), f32)),
        out_specs=(VM, VM, SM),
        name="first_inverse",
        compiler_params=SMALL,
    )(rows_b, rows_c)


def inverse_body(left_ref, right_ref, inverse_ref, penalty_ref):
    penalty_ref[0, 0], inverse_ref[...] = newton_inverse(left_ref[...] * right_ref[...])


def inverse_of(gram_left, gram_right):
    return pl.pallas_call(
        inverse_body,
        out_shape=(jax.ShapeDtypeStruct(gram_left.shape, f32), jax.ShapeDtypeStruct((1, 1), f32)),
        out_specs=(VM, SM),
        name="inverse",
        compiler_params=SMALL,
    )(gram_left, gram_right)


def update_body(sums_ref, start_ref, penalty_ref, inverse_ref, out_ref):
    out_ref[...] = row_update(sums_ref[...], start_ref[...], penalty_ref[0, 0], inverse_ref[...])


def update(sums, start, penalty, inverse):
    return pl.pallas_call(
        update_body,
        in_specs=[VM, VM, SM, VM],
        out_shape=jax.ShapeDtypeStruct(start.shape, bf16),
        out_specs=VM,
        name="update",
        compiler_params=SMALL,
    )(sums, start, penalty, inverse)


def second_update_body(left_ref, right_ref, sums_ref, start_ref, out_ref):
    penalty, inverse = newton_inverse(left_ref[...] * right_ref[...])
    out_ref[...] = row_update(sums_ref[...], start_ref[...], penalty, inverse)


def second_update(gram_left, gram_right, sums, start):
    return pl.pallas_call(
        second_update_body,
        out_shape=jax.ShapeDtypeStruct(start.shape, bf16),
        out_specs=VM,
        name="second_update",
        compiler_params=SMALL,
    )(gram_left, gram_right, sums, start)


def gram_body(rows_ref, out_ref):
    out_ref[...] = gram_of(rows_ref[...])


def gram_call(rows):
    return pl.pallas_call(
        gram_body,
        out_shape=jax.ShapeDtypeStruct((rows.shape[1],) * 2, f32),
        out_specs=VM,
        name="gram",
        compiler_params=SMALL,
    )(rows)


def on_device(sizes, tensor_blocks, block_coords, live_counts, factor_a, factor_b, factor_c):
    nx, ny, nz = sizes
    x_at, y_at, z_at = (lax.axis_index(name) for name in ("gx", "gy", "gz"))
    slot_count, side = tensor_blocks.shape[3], tensor_blocks.shape[4]
    width = factor_a.shape[2]
    blocks = tensor_blocks.reshape(slot_count, side, side, side)
    coords = block_coords.reshape(slot_count * 3)
    live = live_counts.reshape(1)
    own_a, own_b, own_c = factor_a[0], factor_b[0], factor_c[0]
    rows_a, rows_b, rows_c = own_a.shape[0], own_b.shape[0], own_c.shape[0]
    slab = rows_a * ny * nz

    def pick(array, at, axis=0):
        return lax.dynamic_index_in_dim(array, at, axis, keepdims=False)

    def swap_cores(value):
        return lax.ppermute(value, "gz", [(0, 1), (1, 0)])

    def both_cores(value):
        other = swap_cores(value)
        return jnp.where(z_at == 0, jnp.stack([value, other]), jnp.stack([other, value]))

    def spread(value):
        sent = jnp.broadcast_to(value[None], (nx * ny,) + value.shape)
        got = lax.all_to_all(sent, ("gx", "gy"), 0, 0, tiled=True)
        return got.reshape((nx, ny) + value.shape)

    gathered = both_cores(spread(jnp.concatenate([own_b, own_c], axis=0)))
    full_b = gathered[:, :, :, :rows_b].transpose(2, 1, 0, 3, 4).reshape(ny, slab, width)
    full_c = gathered[:, :, :, rows_b:].reshape(nz, slab, width)
    slab_b = jnp.where(y_at == 0, full_b[0], full_b[1]) if ny == 2 else pick(full_b, y_at)
    slab_c = pick(full_c, z_at)

    partial, terms = contract(coords, live, blocks, slab_b, slab_c, 0)
    partial = partial.reshape(ny, nz, rows_a, width)
    sums = pick(partial, z_at, 1) + swap_cores(pick(partial, 1 - z_at, 1))
    sums = sums.reshape(ny * rows_a, width)
    gram_c, inverse, penalty = first_inverse(full_b.reshape(ny * slab, width), full_c.reshape(nz * slab, width))
    if ny == 2:
        height = ny * rows_a
        high = lax.reduce_precision(sums, 8, 7)
        sent = jnp.concatenate([high.astype(bf16), (sums - high).astype(bf16), own_a], axis=0)
        got = lax.ppermute(sent, "gy", [(0, 1), (1, 0)])
        sums = (sent[:height].astype(f32) + sent[height : 2 * height].astype(f32)) + (
            got[:height].astype(f32) + got[height : 2 * height].astype(f32)
        )
        other_a = got[2 * height :]
        start_a = jnp.where(y_at == 0, jnp.concatenate([own_a, other_a]), jnp.concatenate([other_a, own_a]))
    else:
        sums = lax.psum(sums, "gy")
        start_a = lax.all_gather(own_a, "gy", axis=0, tiled=True)
    half_a = update(sums, start_a, penalty, inverse)
    slab_a = both_cores(half_a.reshape(ny, rows_a, width)).transpose(1, 0, 2, 3).reshape(slab, width)
    new_a = pick(half_a.reshape(ny, rows_a, width), y_at)

    partial, gram = second_contract(coords, live, blocks, terms, slab_a, slab_c)
    partial = partial.reshape(nx, nz, rows_b, width)
    share = width // nz
    rows_g = share // nx
    gram_part = lax.dynamic_slice_in_dim(gram, z_at * share, share, 0)
    sums = pick(partial, z_at, 1) + swap_cores(pick(partial, 1 - z_at, 1))

    def pack(sums_rows, gram_rows):
        return jnp.concatenate([sums_rows, gram_rows], axis=-2)

    def unpack(packed):
        return packed[..., :rows_b, :], packed[..., rows_b:, :]

    got = lax.all_to_all(pack(sums, gram_part.reshape(nx, rows_g, width)), "gx", 0, 0, tiled=True)
    sent = jnp.broadcast_to(jnp.sum(got, axis=0)[None], got.shape)
    gathered = both_cores(lax.all_to_all(sent, "gx", 0, 0, tiled=True))
    sums, gram_rows = unpack(gathered)
    gram_a = gram_rows.reshape(width, width)
    sums = sums.transpose(1, 0, 2, 3).reshape(slab, width)
    new_slab_b = second_update(gram_a, gram_c, sums, slab_b)
    new_b = lax.dynamic_slice_in_dim(new_slab_b, (x_at * nz + z_at) * rows_b, rows_b, 0)
    if ny == 2:
        other_b = lax.ppermute(new_slab_b, "gy", [(0, 1), (1, 0)])
        gram_b_new = gram_call(jnp.concatenate([new_slab_b, other_b]))
    else:
        gram_b_new = gram_call(lax.all_gather(new_slab_b, "gy", axis=0, tiled=True))

    (partial,) = contract(coords, live, blocks, slab_a, new_slab_b, 2)
    got = lax.all_to_all(partial.reshape(nx * ny, rows_c, width), ("gx", "gy"), 0, 0, tiled=True)
    inverse, penalty = inverse_of(gram_a, gram_b_new)
    new_c = update(jnp.sum(got.astype(f32), axis=0), own_c, penalty, inverse)
    return new_a[None], new_b[None], new_c[None]


def solution(mesh):
    sizes = tuple(mesh.shape[name] for name in ("gx", "gy", "gz"))
    return jax.shard_map(
        functools.partial(on_device, sizes),
        mesh=mesh,
        in_specs=(
            P("gx", "gy", "gz", None, None, None, None),
            P("gx", "gy", "gz", None, None),
            P("gx", "gy", "gz"),
            P("gx", ("gy", "gz"), None),
            P("gy", ("gx", "gz"), None),
            P("gz", ("gx", "gy"), None),
        ),
        out_specs=(
            P("gx", ("gy", "gz"), None),
            P("gy", ("gx", "gz"), None),
            P("gz", ("gx", "gy"), None),
        ),
        check_vma=False,
    )
```

```python
import functools

import jax
import jax.numpy as jnp
from jax import lax
from jax.experimental import pallas as pl
from jax.experimental.pallas import tpu as pltpu
from jax.sharding import PartitionSpec as P

NS_STEPS = 8
ADMM_ITERS = 4

f32 = jnp.float32
bf16 = jnp.bfloat16

HBM = pl.BlockSpec(memory_space=pltpu.HBM)
VM = pl.BlockSpec(memory_space=pltpu.VMEM)
SM = pl.BlockSpec(memory_space=pltpu.SMEM)

SMALL = pltpu.CompilerParams(vmem_limit_bytes=12 * 2**20)
LARGE = pltpu.CompilerParams(vmem_limit_bytes=53 * 2**20)
FIRST = pltpu.CompilerParams(vmem_limit_bytes=37 * 2**20)
SECOND = pltpu.CompilerParams(vmem_limit_bytes=12 * 2**20)


def split(value):
    high = value.astype(bf16)
    return high, (value - high.astype(f32)).astype(bf16)


def dot3(left, right):
    left_high, left_low = split(left)
    right_high, right_low = split(right)
    mul = functools.partial(jnp.dot, preferred_element_type=f32)
    return mul(left_high, right_high) + (mul(left_low, right_high) + mul(left_high, right_low))


def gram_of(rows):
    return lax.dot_general(rows, rows, (((0,), (0,)), ((), ())), preferred_element_type=f32)


def newton_inverse(weighted):
    width = weighted.shape[0]
    row = lax.broadcasted_iota(jnp.int32, weighted.shape, 0)
    col = lax.broadcasted_iota(jnp.int32, weighted.shape, 1)
    identity = (row == col).astype(f32)
    penalty = jnp.sum(weighted * identity) / width
    system = weighted + penalty * identity
    bound = jnp.max(jnp.sum(jnp.abs(system), axis=1))
    scaled = system / bound
    product = 2.0 * identity - scaled
    scaled = 2.0 * scaled - dot3(scaled, scaled)
    for _ in range(NS_STEPS - 2):
        both = dot3(jnp.concatenate([scaled, product], axis=0), scaled)
        scaled = 2.0 * scaled - both[:width]
        product = 2.0 * product - both[width:]
    product = 2.0 * product - dot3(product, scaled)
    return penalty, product / bound


def row_update(sums, start, penalty, inverse):
    primal = start.astype(f32)
    dual = jnp.zeros_like(primal)
    for _ in range(ADMM_ITERS):
        target = dot3(sums + penalty * (primal + dual), inverse)
        primal = jnp.maximum(target - dual, 0.0)
        dual = dual + primal - target
    return primal.astype(bf16)


def contract_body(chunks, group, out_axis, coords, live, x_hbm, left_ref, right_ref, *refs):
    if out_axis == 0:
        own_hbm, refs, own_ref, own_sem = refs[0], refs[1:], refs[3], refs[4]
        own_copy = pltpu.make_async_copy(own_hbm, own_ref, own_sem)
        own_copy.start()
    out_ref, (x_ref, sem, acc_ref, band_ref) = refs[0], refs[-4:]
    slots, side = x_ref.shape[0], x_ref.shape[1]
    sums_ref = refs[-5] if out_axis == 2 else out_ref

    def copy(slot, n):
        span = pl.ds(*chunks[n])
        return pltpu.make_async_copy(x_hbm.at[slot, span], x_ref.at[slot, span], sem.at[slot, n])

    total = jnp.minimum(live[0], slots)

    def start_copies(step, _):
        for n in range(len(chunks)):
            copy(total - 1 - step, n).start()
        return 0

    def visit(step, _):
        slot = total - 1 - step
        start = [pl.multiple_of(coords[3 * slot + mode] * side, side) for mode in range(3)]
        if out_axis == 0:
            right = right_ref[pl.ds(start[2], side), :]
            band_ref[...] = left_ref[pl.ds(start[1], side), :].astype(f32)
        else:
            right = right_ref[pl.ds(start[3 - out_axis], side), :]
            band_ref[...] = left_ref[pl.ds(start[0], side), :].astype(f32)
            acc_ref[...] = jnp.zeros_like(acc_ref)
        for at in range(0, side, group):
            for n in range(len(chunks)):
                if chunks[n][0] == at:
                    copy(slot, n).wait()
            block = x_ref[slot, at : at + group]
            if out_axis == 2:
                block = jnp.swapaxes(block, 1, 2)
            terms = jnp.dot(block.reshape(group * side, side), right, preferred_element_type=f32)
            terms = terms.reshape(group, side, -1)
            if out_axis == 0:
                refs[1][at : at + group] = terms
                acc_ref[at : at + group, :] = jnp.sum(terms * band_ref[...][None], axis=1)
            else:
                acc_ref[...] += jnp.sum(terms * band_ref[at : at + group, :][:, None, :], axis=0)
        sums_ref[pl.ds(start[out_axis], side), :] += acc_ref[...]
        return 0

    lax.fori_loop(0, total, start_copies, 0)
    sums_ref[...] = jnp.zeros_like(sums_ref)
    lax.fori_loop(0, total, visit, 0)
    if out_axis == 0:
        own_copy.wait()
    if out_axis == 2:
        out_ref[...] = sums_ref[...].astype(out_ref.dtype)


def contract(coords, live, blocks, left, right, out_axis, own=None):
    slots, side = blocks.shape[0], blocks.shape[1]
    group = min(8, side)
    first = side // 4 // group * group or side
    chunks = [(at, size) for at, size in ((0, first), (first, side - first)) if size]
    height, width = left.shape
    outs = [jax.ShapeDtypeStruct((height, width), bf16 if out_axis == 2 else f32)]
    if out_axis == 0:
        outs += [pltpu.VMEM((side, side, width), f32), jax.ShapeDtypeStruct(own.shape, own.dtype)]
    scratch = [
        pltpu.VMEM(blocks.shape, blocks.dtype),
        pltpu.SemaphoreType.DMA((slots, len(chunks))),
        pltpu.VMEM((side, width), f32),
        pltpu.VMEM((side, width), f32),
    ]
    if out_axis == 0:
        scratch = [pltpu.SemaphoreType.DMA] + scratch
    if out_axis == 2:
        scratch = [pltpu.VMEM((height, width), f32)] + scratch
    return pl.pallas_call(
        functools.partial(contract_body, chunks, group, out_axis),
        in_specs=[SM, SM, HBM, VM, VM] + [HBM] * (own is not None),
        out_specs=[VM] * len(outs),
        out_shape=outs,
        scratch_shapes=scratch,
        name=f"contract_{out_axis}",
        compiler_params=FIRST if out_axis == 0 else LARGE,
    )(coords, live, blocks, left, right, *(() if own is None else (own,)))


def second_body(group, coords, live, x_hbm, terms_ref, left_ref, right_ref, out_ref, gram_ref, x_ref, sem, accs_ref, bands_ref):
    side = x_hbm.shape[1]
    total = jnp.minimum(live[0], x_hbm.shape[0])

    def copy(slot):
        return pltpu.make_async_copy(x_hbm.at[slot], x_ref.at[slot - 1], sem.at[slot - 1])

    def start_copy(slot, _):
        copy(slot).start()
        return 0

    lax.fori_loop(1, total, start_copy, 0)
    gram_ref[...] = gram_of(left_ref[...])
    out_ref[...] = jnp.zeros_like(out_ref)

    def open_slot(slot, place):
        start = [pl.multiple_of(coords[3 * slot + mode] * side, side) for mode in range(3)]
        bands_ref[place] = left_ref[pl.ds(start[0], side), :].astype(f32)
        accs_ref[place] = jnp.zeros(accs_ref.shape[1:], f32)
        return start

    def add_kept(at):
        weights = bands_ref[0, at : at + group, :][:, None, :]
        accs_ref[0] += jnp.sum(terms_ref[at : at + group] * weights, axis=0)

    def visit(slot, with_kept):
        start = open_slot(slot, 1)
        right = right_ref[pl.ds(start[2], side), :]
        copy(slot).wait()
        for at in range(0, side, group):
            block = x_ref[slot - 1, at : at + group].reshape(group * side, side)
            terms = jnp.dot(block, right, preferred_element_type=f32).reshape(group, side, -1)
            if with_kept:
                add_kept(at)
            accs_ref[1] += jnp.sum(terms * bands_ref[1, at : at + group, :][:, None, :], axis=0)
        out_ref[pl.ds(start[1], side), :] += accs_ref[1]
        return 0

    first = open_slot(0, 0)

    @pl.when(total == 1)
    def _():
        for at in range(0, side, group):
            add_kept(at)

    @pl.when(total > 1)
    def _():
        visit(1, True)

    out_ref[pl.ds(first[1], side), :] += accs_ref[0]
    lax.fori_loop(2, total, lambda slot, _: visit(slot, False), 0)


def second_contract(coords, live, blocks, terms, left, right):
    slots, side = blocks.shape[0], blocks.shape[1]
    height, width = left.shape
    others = max(slots - 1, 1)
    return pl.pallas_call(
        functools.partial(second_body, min(8, side)),
        in_specs=[SM, SM, HBM, VM, VM, VM],
        out_specs=[VM, VM],
        out_shape=[jax.ShapeDtypeStruct((height, width), f32), jax.ShapeDtypeStruct((width, width), f32)],
        scratch_shapes=[
            pltpu.VMEM((others,) + blocks.shape[1:], blocks.dtype),
            pltpu.SemaphoreType.DMA((others,)),
            pltpu.VMEM((2, side, width), f32),
            pltpu.VMEM((2, side, width), f32),
        ],
        name="contract_1",
        compiler_params=SECOND,
    )(coords, live, blocks, terms, left, right)


def first_inverse_body(b_ref, c_ref, gram_c_ref, inverse_ref, penalty_ref):
    gram_c = gram_of(c_ref[...])
    gram_c_ref[...] = gram_c
    penalty_ref[0, 0], inverse_ref[...] = newton_inverse(gram_of(b_ref[...]) * gram_c)


def first_inverse(rows_b, rows_c):
    square = jax.ShapeDtypeStruct((rows_b.shape[1],) * 2, f32)
    return pl.pallas_call(
        first_inverse_body,
        out_shape=(square, square, jax.ShapeDtypeStruct((1, 1), f32)),
        out_specs=(VM, VM, SM),
        name="first_inverse",
        compiler_params=SMALL,
    )(rows_b, rows_c)


def inverse_body(left_ref, right_ref, inverse_ref, penalty_ref):
    penalty_ref[0, 0], inverse_ref[...] = newton_inverse(left_ref[...] * right_ref[...])


def inverse_of(gram_left, gram_right):
    return pl.pallas_call(
        inverse_body,
        out_shape=(jax.ShapeDtypeStruct(gram_left.shape, f32), jax.ShapeDtypeStruct((1, 1), f32)),
        out_specs=(VM, SM),
        name="inverse",
        compiler_params=SMALL,
    )(gram_left, gram_right)


def update_body(sums_ref, start_ref, penalty_ref, inverse_ref, out_ref):
    out_ref[...] = row_update(sums_ref[...], start_ref[...], penalty_ref[0, 0], inverse_ref[...])


def update(sums, start, penalty, inverse):
    return pl.pallas_call(
        update_body,
        in_specs=[VM, VM, SM, VM],
        out_shape=jax.ShapeDtypeStruct(start.shape, bf16),
        out_specs=VM,
        name="update",
        compiler_params=SMALL,
    )(sums, start, penalty, inverse)


def second_update_body(left_ref, right_ref, sums_ref, start_ref, out_ref):
    penalty, inverse = newton_inverse(left_ref[...] * right_ref[...])
    out_ref[...] = row_update(sums_ref[...], start_ref[...], penalty, inverse)


def second_update(gram_left, gram_right, sums, start):
    return pl.pallas_call(
        second_update_body,
        out_shape=jax.ShapeDtypeStruct(start.shape, bf16),
        out_specs=VM,
        name="second_update",
        compiler_params=SMALL,
    )(gram_left, gram_right, sums, start)


def gram_body(rows_ref, out_ref):
    out_ref[...] = gram_of(rows_ref[...])


def gram_call(rows):
    return pl.pallas_call(
        gram_body,
        out_shape=jax.ShapeDtypeStruct((rows.shape[1],) * 2, f32),
        out_specs=VM,
        name="gram",
        compiler_params=SMALL,
    )(rows)


def on_device(sizes, tensor_blocks, block_coords, live_counts, factor_a, factor_b, factor_c):
    nx, ny, nz = sizes
    x_at, y_at, z_at = (lax.axis_index(name) for name in ("gx", "gy", "gz"))
    slot_count, side = tensor_blocks.shape[3], tensor_blocks.shape[4]
    width = factor_a.shape[2]
    blocks = tensor_blocks.reshape(slot_count, side, side, side)
    coords = block_coords.reshape(slot_count * 3)
    live = live_counts.reshape(1)
    own_a, own_b, own_c = factor_a[0], factor_b[0], factor_c[0]
    rows_a, rows_b, rows_c = own_a.shape[0], own_b.shape[0], own_c.shape[0]
    slab = rows_a * ny * nz

    def pick(array, at, axis=0):
        return lax.dynamic_index_in_dim(array, at, axis, keepdims=False)

    def swap_cores(value):
        return lax.ppermute(value, "gz", [(0, 1), (1, 0)])

    def both_cores(value):
        other = swap_cores(value)
        return jnp.where(z_at == 0, jnp.stack([value, other]), jnp.stack([other, value]))

    def spread(value):
        sent = jnp.broadcast_to(value[None], (nx * ny,) + value.shape)
        got = lax.all_to_all(sent, ("gx", "gy"), 0, 0, tiled=True)
        return got.reshape((nx, ny) + value.shape)

    gathered = both_cores(spread(jnp.concatenate([own_b, own_c], axis=0)))
    full_b = gathered[:, :, :, :rows_b].transpose(2, 1, 0, 3, 4).reshape(ny, slab, width)
    full_c = gathered[:, :, :, rows_b:].reshape(nz, slab, width)
    slab_b = jnp.where(y_at == 0, full_b[0], full_b[1]) if ny == 2 else pick(full_b, y_at)
    slab_c = pick(full_c, z_at)

    partial, terms, own_a = contract(coords, live, blocks, slab_b, slab_c, 0, own_a)
    partial = partial.reshape(ny, nz, rows_a, width)
    sums = pick(partial, z_at, 1) + swap_cores(pick(partial, 1 - z_at, 1))
    sums = sums.reshape(ny * rows_a, width)
    gram_c, inverse, penalty = first_inverse(full_b.reshape(ny * slab, width), full_c.reshape(nz * slab, width))
    if ny == 2:
        height = ny * rows_a
        high = lax.reduce_precision(sums, 8, 7)
        sent = jnp.concatenate([high.astype(bf16), (sums - high).astype(bf16), own_a], axis=0)
        got = lax.ppermute(sent, "gy", [(0, 1), (1, 0)])
        sums = (sent[:height].astype(f32) + sent[height : 2 * height].astype(f32)) + (
            got[:height].astype(f32) + got[height : 2 * height].astype(f32)
        )
        other_a = got[2 * height :]
        start_a = jnp.where(y_at == 0, jnp.concatenate([own_a, other_a]), jnp.concatenate([other_a, own_a]))
    else:
        sums = lax.psum(sums, "gy")
        start_a = lax.all_gather(own_a, "gy", axis=0, tiled=True)
    half_a = update(sums, start_a, penalty, inverse)
    slab_a = both_cores(half_a.reshape(ny, rows_a, width)).transpose(1, 0, 2, 3).reshape(slab, width)
    new_a = pick(half_a.reshape(ny, rows_a, width), y_at)

    partial, gram = second_contract(coords, live, blocks, terms, slab_a, slab_c)
    partial = partial.reshape(nx, nz, rows_b, width)
    share = width // nz
    rows_g = share // nx
    gram_part = lax.dynamic_slice_in_dim(gram, z_at * share, share, 0)
    sums = pick(partial, z_at, 1) + swap_cores(pick(partial, 1 - z_at, 1))

    def pack(sums_rows, gram_rows):
        return jnp.concatenate([sums_rows, gram_rows], axis=-2)

    def unpack(packed):
        return packed[..., :rows_b, :], packed[..., rows_b:, :]

    got = lax.all_to_all(pack(sums, gram_part.reshape(nx, rows_g, width)), "gx", 0, 0, tiled=True)
    sent = jnp.broadcast_to(jnp.sum(got, axis=0)[None], got.shape)
    gathered = both_cores(lax.all_to_all(sent, "gx", 0, 0, tiled=True))
    sums, gram_rows = unpack(gathered)
    gram_a = gram_rows.reshape(width, width)
    sums = sums.transpose(1, 0, 2, 3).reshape(slab, width)
    new_slab_b = second_update(gram_a, gram_c, sums, slab_b)
    new_b = lax.dynamic_slice_in_dim(new_slab_b, (x_at * nz + z_at) * rows_b, rows_b, 0)
    if ny == 2:
        other_b = lax.ppermute(new_slab_b, "gy", [(0, 1), (1, 0)])
        gram_b_new = gram_call(jnp.concatenate([new_slab_b, other_b]))
    else:
        gram_b_new = gram_call(lax.all_gather(new_slab_b, "gy", axis=0, tiled=True))

    (partial,) = contract(coords, live, blocks, slab_a, new_slab_b, 2)
    got = lax.all_to_all(partial.reshape(nx * ny, rows_c, width), ("gx", "gy"), 0, 0, tiled=True)
    inverse, penalty = inverse_of(gram_a, gram_b_new)
    new_c = update(jnp.sum(got.astype(f32), axis=0), own_c, penalty, inverse)
    return new_a[None], new_b[None], new_c[None]


def solution(mesh):
    sizes = tuple(mesh.shape[name] for name in ("gx", "gy", "gz"))
    return jax.shard_map(
        functools.partial(on_device, sizes),
        mesh=mesh,
        in_specs=(
            P("gx", "gy", "gz", None, None, None, None),
            P("gx", "gy", "gz", None, None),
            P("gx", "gy", "gz"),
            P("gx", ("gy", "gz"), None),
            P("gy", ("gx", "gz"), None),
            P("gz", ("gx", "gy"), None),
        ),
        out_specs=(
            P("gx", ("gy", "gz"), None),
            P("gy", ("gx", "gz"), None),
            P("gz", ("gx", "gy"), None),
        ),
        check_vma=False,
    )
```

```python
import functools

import jax
import jax.numpy as jnp
from jax import lax
from jax.experimental import pallas as pl
from jax.experimental.pallas import tpu as pltpu
from jax.sharding import PartitionSpec as P

NS_STEPS = 8
ADMM_ITERS = 4

f32 = jnp.float32
bf16 = jnp.bfloat16

HBM = pl.BlockSpec(memory_space=pltpu.HBM)
VM = pl.BlockSpec(memory_space=pltpu.VMEM)
SM = pl.BlockSpec(memory_space=pltpu.SMEM)

SMALL = pltpu.CompilerParams(vmem_limit_bytes=12 * 2**20)
LARGE = pltpu.CompilerParams(vmem_limit_bytes=53 * 2**20)
FIRST = pltpu.CompilerParams(vmem_limit_bytes=37 * 2**20)
SECOND = pltpu.CompilerParams(vmem_limit_bytes=12 * 2**20)


def split(value):
    high = value.astype(bf16)
    return high, (value - high.astype(f32)).astype(bf16)


def dot3(left, right):
    left_high, left_low = split(left)
    right_high, right_low = split(right)
    mul = functools.partial(jnp.dot, preferred_element_type=f32)
    return mul(left_high, right_high) + (mul(left_low, right_high) + mul(left_high, right_low))


def gram_of(rows):
    return lax.dot_general(rows, rows, (((0,), (0,)), ((), ())), preferred_element_type=f32)


def newton_inverse(weighted):
    width = weighted.shape[0]
    row = lax.broadcasted_iota(jnp.int32, weighted.shape, 0)
    col = lax.broadcasted_iota(jnp.int32, weighted.shape, 1)
    identity = (row == col).astype(f32)
    penalty = jnp.sum(weighted * identity) / width
    system = weighted + penalty * identity
    bound = jnp.max(jnp.sum(jnp.abs(system), axis=1))
    scaled = system / bound
    product = 2.0 * identity - scaled
    scaled = 2.0 * scaled - dot3(scaled, scaled)
    for _ in range(NS_STEPS - 2):
        both = dot3(jnp.concatenate([scaled, product], axis=0), scaled)
        scaled = 2.0 * scaled - both[:width]
        product = 2.0 * product - both[width:]
    product = 2.0 * product - dot3(product, scaled)
    return penalty, product / bound


def row_update(sums, start, penalty, inverse):
    primal = start.astype(f32)
    dual = jnp.zeros_like(primal)
    for _ in range(ADMM_ITERS):
        target = dot3(sums + penalty * (primal + dual), inverse)
        primal = jnp.maximum(target - dual, 0.0)
        dual = dual + primal - target
    return primal.astype(bf16)


def own_rows(inner_axes, slab_ref, own_hbm, sem):
    rows = own_hbm.shape[0]
    at = 0
    for name, size in inner_axes:
        at = at * size + lax.axis_index(name)
    return pltpu.make_async_copy(slab_ref.at[pl.ds(pl.multiple_of(at * rows, rows), rows)], own_hbm, sem)


def contract_body(chunks, group, out_axis, inner_axes, coords, live, x_hbm, left_ref, right_ref, *refs):
    if out_axis == 2:
        refs, own_hbm, own_sem = (refs[0],) + refs[3:], refs[1], refs[2]
        own_copy = own_rows(inner_axes, right_ref, own_hbm, own_sem)
        own_copy.start()
    if out_axis == 0:
        own_hbm, refs, own_ref, own_sem = refs[0], refs[1:], refs[3], refs[4]
        own_copy = pltpu.make_async_copy(own_hbm, own_ref, own_sem)
        own_copy.start()
    out_ref, (x_ref, sem, acc_ref, band_ref) = refs[0], refs[-4:]
    slots, side = x_ref.shape[0], x_ref.shape[1]
    sums_ref = refs[-5] if out_axis == 2 else out_ref

    def copy(slot, n):
        span = pl.ds(*chunks[n])
        return pltpu.make_async_copy(x_hbm.at[slot, span], x_ref.at[slot, span], sem.at[slot, n])

    total = jnp.minimum(live[0], slots)

    def start_copies(step, _):
        for n in range(len(chunks)):
            copy(total - 1 - step, n).start()
        return 0

    def visit(step, _):
        slot = total - 1 - step
        start = [pl.multiple_of(coords[3 * slot + mode] * side, side) for mode in range(3)]
        if out_axis == 0:
            right = right_ref[pl.ds(start[2], side), :]
            band_ref[...] = left_ref[pl.ds(start[1], side), :].astype(f32)
        else:
            right = right_ref[pl.ds(start[3 - out_axis], side), :]
            band_ref[...] = left_ref[pl.ds(start[0], side), :].astype(f32)
            acc_ref[...] = jnp.zeros_like(acc_ref)
        for at in range(0, side, group):
            for n in range(len(chunks)):
                if chunks[n][0] == at:
                    copy(slot, n).wait()
            block = x_ref[slot, at : at + group]
            if out_axis == 2:
                block = jnp.swapaxes(block, 1, 2)
            terms = jnp.dot(block.reshape(group * side, side), right, preferred_element_type=f32)
            terms = terms.reshape(group, side, -1)
            if out_axis == 0:
                refs[1][at : at + group] = terms
                acc_ref[at : at + group, :] = jnp.sum(terms * band_ref[...][None], axis=1)
            else:
                acc_ref[...] += jnp.sum(terms * band_ref[at : at + group, :][:, None, :], axis=0)
        sums_ref[pl.ds(start[out_axis], side), :] += acc_ref[...]
        return 0

    lax.fori_loop(0, total, start_copies, 0)
    sums_ref[...] = jnp.zeros_like(sums_ref)
    lax.fori_loop(0, total, visit, 0)
    own_copy.wait()
    if out_axis == 2:
        out_ref[...] = sums_ref[...].astype(out_ref.dtype)


def contract(coords, live, blocks, left, right, out_axis, own, inner_axes=()):
    slots, side = blocks.shape[0], blocks.shape[1]
    group = min(8, side)
    first = side // 4 // group * group or side
    chunks = [(at, size) for at, size in ((0, first), (first, side - first)) if size]
    height, width = left.shape
    outs = [jax.ShapeDtypeStruct((height, width), bf16 if out_axis == 2 else f32)]
    if out_axis == 0:
        outs += [pltpu.VMEM((side, side, width), f32), jax.ShapeDtypeStruct(own.shape, own.dtype)]
    scratch = [
        pltpu.VMEM(blocks.shape, blocks.dtype),
        pltpu.SemaphoreType.DMA((slots, len(chunks))),
        pltpu.VMEM((side, width), f32),
        pltpu.VMEM((side, width), f32),
    ]
    if out_axis == 0:
        scratch = [pltpu.SemaphoreType.DMA] + scratch
    if out_axis == 2:
        outs.append(jax.ShapeDtypeStruct(own.shape, own.dtype))
        scratch = [pltpu.SemaphoreType.DMA, pltpu.VMEM((height, width), f32)] + scratch
    return pl.pallas_call(
        functools.partial(contract_body, chunks, group, out_axis, inner_axes),
        in_specs=[SM, SM, HBM, VM, VM] + [HBM] * (out_axis == 0),
        out_specs=[VM] * len(outs) if out_axis == 0 else [VM, HBM],
        out_shape=outs,
        scratch_shapes=scratch,
        name=f"contract_{out_axis}",
        compiler_params=FIRST if out_axis == 0 else LARGE,
    )(coords, live, blocks, left, right, *((own,) if out_axis == 0 else ()))


def second_body(
    group, inner_axes, coords, live, x_hbm, terms_ref, left_ref, right_ref, out_ref, gram_ref, own_hbm,
    x_ref, sem, own_sem, accs_ref, bands_ref,
):
    side = x_hbm.shape[1]
    total = jnp.minimum(live[0], x_hbm.shape[0])

    def copy(slot):
        return pltpu.make_async_copy(x_hbm.at[slot], x_ref.at[slot - 1], sem.at[slot - 1])

    def start_copy(slot, _):
        copy(slot).start()
        return 0

    lax.fori_loop(1, total, start_copy, 0)
    own_copy = own_rows(inner_axes, left_ref, own_hbm, own_sem)
    own_copy.start()
    gram_ref[...] = gram_of(left_ref[...])
    out_ref[...] = jnp.zeros_like(out_ref)

    def open_slot(slot, place):
        start = [pl.multiple_of(coords[3 * slot + mode] * side, side) for mode in range(3)]
        bands_ref[place] = left_ref[pl.ds(start[0], side), :].astype(f32)
        accs_ref[place] = jnp.zeros(accs_ref.shape[1:], f32)
        return start

    def add_kept(at):
        weights = bands_ref[0, at : at + group, :][:, None, :]
        accs_ref[0] += jnp.sum(terms_ref[at : at + group] * weights, axis=0)

    def visit(slot, with_kept):
        start = open_slot(slot, 1)
        right = right_ref[pl.ds(start[2], side), :]
        copy(slot).wait()
        for at in range(0, side, group):
            block = x_ref[slot - 1, at : at + group].reshape(group * side, side)
            terms = jnp.dot(block, right, preferred_element_type=f32).reshape(group, side, -1)
            if with_kept:
                add_kept(at)
            accs_ref[1] += jnp.sum(terms * bands_ref[1, at : at + group, :][:, None, :], axis=0)
        out_ref[pl.ds(start[1], side), :] += accs_ref[1]
        return 0

    first = open_slot(0, 0)

    @pl.when(total == 1)
    def _():
        for at in range(0, side, group):
            add_kept(at)

    @pl.when(total > 1)
    def _():
        visit(1, True)

    out_ref[pl.ds(first[1], side), :] += accs_ref[0]
    lax.fori_loop(2, total, lambda slot, _: visit(slot, False), 0)
    own_copy.wait()


def second_contract(coords, live, blocks, terms, left, right, own, inner_axes):
    slots, side = blocks.shape[0], blocks.shape[1]
    height, width = left.shape
    others = max(slots - 1, 1)
    return pl.pallas_call(
        functools.partial(second_body, min(8, side), inner_axes),
        in_specs=[SM, SM, HBM, VM, VM, VM],
        out_specs=[VM, VM, HBM],
        out_shape=[
            jax.ShapeDtypeStruct((height, width), f32),
            jax.ShapeDtypeStruct((width, width), f32),
            jax.ShapeDtypeStruct(own.shape, own.dtype),
        ],
        scratch_shapes=[
            pltpu.VMEM((others,) + blocks.shape[1:], blocks.dtype),
            pltpu.SemaphoreType.DMA((others,)),
            pltpu.SemaphoreType.DMA,
            pltpu.VMEM((2, side, width), f32),
            pltpu.VMEM((2, side, width), f32),
        ],
        name="contract_1",
        compiler_params=SECOND,
    )(coords, live, blocks, terms, left, right)


def first_inverse_body(b_ref, c_ref, gram_c_ref, inverse_ref, penalty_ref):
    gram_c = gram_of(c_ref[...])
    gram_c_ref[...] = gram_c
    penalty_ref[0, 0], inverse_ref[...] = newton_inverse(gram_of(b_ref[...]) * gram_c)


def first_inverse(rows_b, rows_c):
    square = jax.ShapeDtypeStruct((rows_b.shape[1],) * 2, f32)
    return pl.pallas_call(
        first_inverse_body,
        out_shape=(square, square, jax.ShapeDtypeStruct((1, 1), f32)),
        out_specs=(VM, VM, SM),
        name="first_inverse",
        compiler_params=SMALL,
    )(rows_b, rows_c)


def inverse_body(left_ref, right_ref, inverse_ref, penalty_ref):
    penalty_ref[0, 0], inverse_ref[...] = newton_inverse(left_ref[...] * right_ref[...])


def inverse_of(gram_left, gram_right):
    return pl.pallas_call(
        inverse_body,
        out_shape=(jax.ShapeDtypeStruct(gram_left.shape, f32), jax.ShapeDtypeStruct((1, 1), f32)),
        out_specs=(VM, SM),
        name="inverse",
        compiler_params=SMALL,
    )(gram_left, gram_right)


def update_body(sums_ref, start_ref, penalty_ref, inverse_ref, out_ref):
    out_ref[...] = row_update(sums_ref[...], start_ref[...], penalty_ref[0, 0], inverse_ref[...])


def update(sums, start, penalty, inverse):
    return pl.pallas_call(
        update_body,
        in_specs=[VM, VM, SM, VM],
        out_shape=jax.ShapeDtypeStruct(start.shape, bf16),
        out_specs=VM,
        name="update",
        compiler_params=SMALL,
    )(sums, start, penalty, inverse)


def second_update_body(left_ref, right_ref, sums_ref, start_ref, out_ref):
    penalty, inverse = newton_inverse(left_ref[...] * right_ref[...])
    out_ref[...] = row_update(sums_ref[...], start_ref[...], penalty, inverse)


def second_update(gram_left, gram_right, sums, start):
    return pl.pallas_call(
        second_update_body,
        out_shape=jax.ShapeDtypeStruct(start.shape, bf16),
        out_specs=VM,
        name="second_update",
        compiler_params=SMALL,
    )(gram_left, gram_right, sums, start)


def gram_body(rows_ref, out_ref):
    out_ref[...] = gram_of(rows_ref[...])


def gram_call(rows):
    return pl.pallas_call(
        gram_body,
        out_shape=jax.ShapeDtypeStruct((rows.shape[1],) * 2, f32),
        out_specs=VM,
        name="gram",
        compiler_params=SMALL,
    )(rows)


def on_device(sizes, tensor_blocks, block_coords, live_counts, factor_a, factor_b, factor_c):
    nx, ny, nz = sizes
    y_at, z_at = lax.axis_index("gy"), lax.axis_index("gz")
    slot_count, side = tensor_blocks.shape[3], tensor_blocks.shape[4]
    width = factor_a.shape[2]
    blocks = tensor_blocks.reshape(slot_count, side, side, side)
    coords = block_coords.reshape(slot_count * 3)
    live = live_counts.reshape(1)
    own_a, own_b, own_c = factor_a[0], factor_b[0], factor_c[0]
    rows_a, rows_b, rows_c = own_a.shape[0], own_b.shape[0], own_c.shape[0]
    slab = rows_a * ny * nz

    def pick(array, at, axis=0):
        return lax.dynamic_index_in_dim(array, at, axis, keepdims=False)

    def swap_cores(value):
        return lax.ppermute(value, "gz", [(0, 1), (1, 0)])

    def both_cores(value):
        other = swap_cores(value)
        return jnp.where(z_at == 0, jnp.stack([value, other]), jnp.stack([other, value]))

    def spread(value):
        sent = jnp.broadcast_to(value[None], (nx * ny,) + value.shape)
        got = lax.all_to_all(sent, ("gx", "gy"), 0, 0, tiled=True)
        return got.reshape((nx, ny) + value.shape)

    gathered = both_cores(spread(jnp.concatenate([own_b, own_c], axis=0)))
    full_b = gathered[:, :, :, :rows_b].transpose(2, 1, 0, 3, 4).reshape(ny, slab, width)
    full_c = gathered[:, :, :, rows_b:].reshape(nz, slab, width)
    slab_b = jnp.where(y_at == 0, full_b[0], full_b[1]) if ny == 2 else pick(full_b, y_at)
    slab_c = pick(full_c, z_at)

    partial, terms, own_a = contract(coords, live, blocks, slab_b, slab_c, 0, own_a)
    partial = partial.reshape(ny, nz, rows_a, width)
    sums = pick(partial, z_at, 1) + swap_cores(pick(partial, 1 - z_at, 1))
    sums = sums.reshape(ny * rows_a, width)
    gram_c, inverse, penalty = first_inverse(full_b.reshape(ny * slab, width), full_c.reshape(nz * slab, width))
    if ny == 2:
        height = ny * rows_a
        high = lax.reduce_precision(sums, 8, 7)
        sent = jnp.concatenate([high.astype(bf16), (sums - high).astype(bf16), own_a], axis=0)
        got = lax.ppermute(sent, "gy", [(0, 1), (1, 0)])
        sums = (sent[:height].astype(f32) + sent[height : 2 * height].astype(f32)) + (
            got[:height].astype(f32) + got[height : 2 * height].astype(f32)
        )
        other_a = got[2 * height :]
        start_a = jnp.where(y_at == 0, jnp.concatenate([own_a, other_a]), jnp.concatenate([other_a, own_a]))
    else:
        sums = lax.psum(sums, "gy")
        start_a = lax.all_gather(own_a, "gy", axis=0, tiled=True)
    half_a = update(sums, start_a, penalty, inverse)
    slab_a = both_cores(half_a.reshape(ny, rows_a, width)).transpose(1, 0, 2, 3).reshape(slab, width)

    inner_axes = (("gy", ny), ("gz", nz))
    partial, gram, new_a = second_contract(coords, live, blocks, terms, slab_a, slab_c, own_a, inner_axes)
    partial = partial.reshape(nx, nz, rows_b, width)
    share = width // nz
    rows_g = share // nx
    gram_part = lax.dynamic_slice_in_dim(gram, z_at * share, share, 0)
    sums = pick(partial, z_at, 1) + swap_cores(pick(partial, 1 - z_at, 1))

    def pack(sums_rows, gram_rows):
        return jnp.concatenate([sums_rows, gram_rows], axis=-2)

    def unpack(packed):
        return packed[..., :rows_b, :], packed[..., rows_b:, :]

    got = lax.all_to_all(pack(sums, gram_part.reshape(nx, rows_g, width)), "gx", 0, 0, tiled=True)
    sent = jnp.broadcast_to(jnp.sum(got, axis=0)[None], got.shape)
    gathered = both_cores(lax.all_to_all(sent, "gx", 0, 0, tiled=True))
    sums, gram_rows = unpack(gathered)
    gram_a = gram_rows.reshape(width, width)
    sums = sums.transpose(1, 0, 2, 3).reshape(slab, width)
    new_slab_b = second_update(gram_a, gram_c, sums, slab_b)
    if ny == 2:
        other_b = lax.ppermute(new_slab_b, "gy", [(0, 1), (1, 0)])
        gram_b_new = gram_call(jnp.concatenate([new_slab_b, other_b]))
    else:
        gram_b_new = gram_call(lax.all_gather(new_slab_b, "gy", axis=0, tiled=True))

    inner_axes = (("gx", nx), ("gz", nz))
    partial, new_b = contract(coords, live, blocks, slab_a, new_slab_b, 2, own_b, inner_axes)
    got = lax.all_to_all(partial.reshape(nx * ny, rows_c, width), ("gx", "gy"), 0, 0, tiled=True)
    inverse, penalty = inverse_of(gram_a, gram_b_new)
    new_c = update(jnp.sum(got.astype(f32), axis=0), own_c, penalty, inverse)
    return new_a[None], new_b[None], new_c[None]


def solution(mesh):
    sizes = tuple(mesh.shape[name] for name in ("gx", "gy", "gz"))
    return jax.shard_map(
        functools.partial(on_device, sizes),
        mesh=mesh,
        in_specs=(
            P("gx", "gy", "gz", None, None, None, None),
            P("gx", "gy", "gz", None, None),
            P("gx", "gy", "gz"),
            P("gx", ("gy", "gz"), None),
            P("gy", ("gx", "gz"), None),
            P("gz", ("gx", "gy"), None),
        ),
        out_specs=(
            P("gx", ("gy", "gz"), None),
            P("gy", ("gx", "gz"), None),
            P("gz", ("gx", "gy"), None),
        ),
        check_vma=False,
    )
```

```python
import functools

import jax
import jax.numpy as jnp
from jax import lax
from jax.experimental import pallas as pl
from jax.experimental.pallas import tpu as pltpu
from jax.sharding import PartitionSpec as P

NS_STEPS = 8
ADMM_ITERS = 4

f32 = jnp.float32
bf16 = jnp.bfloat16

HBM = pl.BlockSpec(memory_space=pltpu.HBM)
VM = pl.BlockSpec(memory_space=pltpu.VMEM)
SM = pl.BlockSpec(memory_space=pltpu.SMEM)

SMALL = pltpu.CompilerParams(vmem_limit_bytes=12 * 2**20)
LARGE = pltpu.CompilerParams(vmem_limit_bytes=53 * 2**20)
FIRST = pltpu.CompilerParams(vmem_limit_bytes=37 * 2**20)
SECOND = pltpu.CompilerParams(vmem_limit_bytes=12 * 2**20)


def split(value):
    high = value.astype(bf16)
    return high, (value - high.astype(f32)).astype(bf16)


def dot3(left, right):
    left_high, left_low = split(left)
    right_high, right_low = split(right)
    mul = functools.partial(jnp.dot, preferred_element_type=f32)
    return mul(left_high, right_high) + (mul(left_low, right_high) + mul(left_high, right_low))


def gram_of(rows):
    return lax.dot_general(rows, rows, (((0,), (0,)), ((), ())), preferred_element_type=f32)


def newton_inverse(weighted):
    width = weighted.shape[0]
    row = lax.broadcasted_iota(jnp.int32, weighted.shape, 0)
    col = lax.broadcasted_iota(jnp.int32, weighted.shape, 1)
    identity = (row == col).astype(f32)
    penalty = jnp.sum(weighted * identity) / width
    system = weighted + penalty * identity
    bound = jnp.max(jnp.sum(jnp.abs(system), axis=1))
    scaled = system / bound
    product = 2.0 * identity - scaled
    scaled = 2.0 * scaled - dot3(scaled, scaled)
    for _ in range(NS_STEPS - 2):
        both = dot3(jnp.concatenate([scaled, product], axis=0), scaled)
        scaled = 2.0 * scaled - both[:width]
        product = 2.0 * product - both[width:]
    product = 2.0 * product - dot3(product, scaled)
    return penalty, product / bound


def row_update(sums, start, penalty, inverse):
    primal = start.astype(f32)
    dual = jnp.zeros_like(primal)
    for _ in range(ADMM_ITERS):
        target = dot3(sums + penalty * (primal + dual), inverse)
        primal = jnp.maximum(target - dual, 0.0)
        dual = dual + primal - target
    return primal.astype(bf16)


def cuts(side):
    group = min(8, side)
    first = side // 4 // group * group or side
    return group, [(at, size) for at, size in ((0, first), (first, side - first)) if size]


def own_rows(inner_axes, slab_ref, own_hbm, sem):
    rows = own_hbm.shape[0]
    at = 0
    for name, size in inner_axes:
        at = at * size + lax.axis_index(name)
    return pltpu.make_async_copy(slab_ref.at[pl.ds(pl.multiple_of(at * rows, rows), rows)], own_hbm, sem)


def contract_body(chunks, group, out_axis, inner_axes, coords, live, x_hbm, left_ref, right_ref, *refs):
    if out_axis == 2:
        refs, own_hbm, own_sem = (refs[0],) + refs[3:], refs[1], refs[2]
        own_copy = own_rows(inner_axes, right_ref, own_hbm, own_sem)
        own_copy.start()
    if out_axis == 0:
        own_hbm, refs, own_ref, own_sem = refs[0], refs[1:], refs[3], refs[4]
        own_copy = pltpu.make_async_copy(own_hbm, own_ref, own_sem)
        own_copy.start()
    out_ref, (x_ref, sem, acc_ref, band_ref) = refs[0], refs[-4:]
    slots, side = x_ref.shape[0], x_ref.shape[1]
    sums_ref = refs[-5] if out_axis == 2 else out_ref

    def copy(slot, n):
        span = pl.ds(*chunks[n])
        return pltpu.make_async_copy(x_hbm.at[slot, span], x_ref.at[slot, span], sem.at[slot, n])

    total = jnp.minimum(live[0], slots)

    def start_copies(step, _):
        for n in range(len(chunks)):
            copy(total - 1 - step, n).start()
        return 0

    def visit(step, _):
        slot = total - 1 - step
        start = [pl.multiple_of(coords[3 * slot + mode] * side, side) for mode in range(3)]
        if out_axis == 0:
            right = right_ref[pl.ds(start[2], side), :]
            band_ref[...] = left_ref[pl.ds(start[1], side), :].astype(f32)
        else:
            right = right_ref[pl.ds(start[3 - out_axis], side), :]
            band_ref[...] = left_ref[pl.ds(start[0], side), :].astype(f32)
            acc_ref[...] = jnp.zeros_like(acc_ref)
        for at in range(0, side, group):
            for n in range(len(chunks)):
                if chunks[n][0] == at:
                    copy(slot, n).wait()
            block = x_ref[slot, at : at + group]
            if out_axis == 2:
                block = jnp.swapaxes(block, 1, 2)
            terms = jnp.dot(block.reshape(group * side, side), right, preferred_element_type=f32)
            terms = terms.reshape(group, side, -1)
            if out_axis == 0:
                refs[1][at : at + group] = terms
                acc_ref[at : at + group, :] = jnp.sum(terms * band_ref[...][None], axis=1)
            else:
                acc_ref[...] += jnp.sum(terms * band_ref[at : at + group, :][:, None, :], axis=0)
        sums_ref[pl.ds(start[out_axis], side), :] += acc_ref[...]
        return 0

    lax.fori_loop(0, total, start_copies, 0)
    sums_ref[...] = jnp.zeros_like(sums_ref)
    lax.fori_loop(0, total, visit, 0)
    own_copy.wait()
    if out_axis == 2:
        out_ref[...] = sums_ref[...].astype(out_ref.dtype)


def contract(coords, live, blocks, left, right, out_axis, own, inner_axes=()):
    slots, side = blocks.shape[0], blocks.shape[1]
    group, chunks = cuts(side)
    height, width = left.shape
    outs = [jax.ShapeDtypeStruct((height, width), bf16 if out_axis == 2 else f32)]
    if out_axis == 0:
        outs += [pltpu.VMEM((side, side, width), f32), jax.ShapeDtypeStruct(own.shape, own.dtype)]
    scratch = [
        pltpu.VMEM(blocks.shape, blocks.dtype),
        pltpu.SemaphoreType.DMA((slots, len(chunks))),
        pltpu.VMEM((side, width), f32),
        pltpu.VMEM((side, width), f32),
    ]
    if out_axis == 0:
        scratch = [pltpu.SemaphoreType.DMA] + scratch
    if out_axis == 2:
        outs.append(jax.ShapeDtypeStruct(own.shape, own.dtype))
        scratch = [pltpu.SemaphoreType.DMA, pltpu.VMEM((height, width), f32)] + scratch
    return pl.pallas_call(
        functools.partial(contract_body, chunks, group, out_axis, inner_axes),
        in_specs=[SM, SM, HBM, VM, VM] + [HBM] * (out_axis == 0),
        out_specs=[VM] * len(outs) if out_axis == 0 else [VM, HBM],
        out_shape=outs,
        scratch_shapes=scratch,
        name=f"contract_{out_axis}",
        compiler_params=FIRST if out_axis == 0 else LARGE,
    )(coords, live, blocks, left, right, *((own,) if out_axis == 0 else ()))


def second_body(
    chunks, group, inner_axes, coords, live, x_hbm, terms_ref, left_ref, right_ref, out_ref, gram_ref, own_hbm,
    x_ref, sem, own_sem, accs_ref, bands_ref,
):
    side = x_hbm.shape[1]
    total = jnp.minimum(live[0], x_hbm.shape[0])

    def copy(slot, n):
        span = pl.ds(*chunks[n])
        return pltpu.make_async_copy(x_hbm.at[slot, span], x_ref.at[slot - 1, span], sem.at[slot - 1, n])

    def start_copy(slot, _):
        for n in range(len(chunks)):
            copy(slot, n).start()
        return 0

    lax.fori_loop(1, total, start_copy, 0)
    own_copy = own_rows(inner_axes, left_ref, own_hbm, own_sem)
    own_copy.start()
    gram_ref[...] = gram_of(left_ref[...])
    out_ref[...] = jnp.zeros_like(out_ref)

    def open_slot(slot, place):
        start = [pl.multiple_of(coords[3 * slot + mode] * side, side) for mode in range(3)]
        bands_ref[place] = left_ref[pl.ds(start[0], side), :].astype(f32)
        accs_ref[place] = jnp.zeros(accs_ref.shape[1:], f32)
        return start

    def add_kept(at):
        weights = bands_ref[0, at : at + group, :][:, None, :]
        accs_ref[0] += jnp.sum(terms_ref[at : at + group] * weights, axis=0)

    def visit(slot, with_kept):
        start = open_slot(slot, 1)
        right = right_ref[pl.ds(start[2], side), :]
        for at in range(0, side, group):
            for n in range(len(chunks)):
                if chunks[n][0] == at:
                    copy(slot, n).wait()
            block = x_ref[slot - 1, at : at + group].reshape(group * side, side)
            terms = jnp.dot(block, right, preferred_element_type=f32).reshape(group, side, -1)
            if with_kept:
                add_kept(at)
            accs_ref[1] += jnp.sum(terms * bands_ref[1, at : at + group, :][:, None, :], axis=0)
        out_ref[pl.ds(start[1], side), :] += accs_ref[1]
        return 0

    first = open_slot(0, 0)

    @pl.when(total == 1)
    def _():
        for at in range(0, side, group):
            add_kept(at)

    @pl.when(total > 1)
    def _():
        visit(1, True)

    out_ref[pl.ds(first[1], side), :] += accs_ref[0]
    lax.fori_loop(2, total, lambda slot, _: visit(slot, False), 0)
    own_copy.wait()


def second_contract(coords, live, blocks, terms, left, right, own, inner_axes):
    slots, side = blocks.shape[0], blocks.shape[1]
    height, width = left.shape
    others = max(slots - 1, 1)
    group, chunks = cuts(side)
    return pl.pallas_call(
        functools.partial(second_body, chunks, group, inner_axes),
        in_specs=[SM, SM, HBM, VM, VM, VM],
        out_specs=[VM, VM, HBM],
        out_shape=[
            jax.ShapeDtypeStruct((height, width), f32),
            jax.ShapeDtypeStruct((width, width), f32),
            jax.ShapeDtypeStruct(own.shape, own.dtype),
        ],
        scratch_shapes=[
            pltpu.VMEM((others,) + blocks.shape[1:], blocks.dtype),
            pltpu.SemaphoreType.DMA((others, len(chunks))),
            pltpu.SemaphoreType.DMA,
            pltpu.VMEM((2, side, width), f32),
            pltpu.VMEM((2, side, width), f32),
        ],
        name="contract_1",
        compiler_params=SECOND,
    )(coords, live, blocks, terms, left, right)


def first_inverse_body(b_ref, c_ref, gram_c_ref, inverse_ref, penalty_ref):
    gram_c = gram_of(c_ref[...])
    gram_c_ref[...] = gram_c
    penalty_ref[0, 0], inverse_ref[...] = newton_inverse(gram_of(b_ref[...]) * gram_c)


def first_inverse(rows_b, rows_c):
    square = jax.ShapeDtypeStruct((rows_b.shape[1],) * 2, f32)
    return pl.pallas_call(
        first_inverse_body,
        out_shape=(square, square, jax.ShapeDtypeStruct((1, 1), f32)),
        out_specs=(VM, VM, SM),
        name="first_inverse",
        compiler_params=SMALL,
    )(rows_b, rows_c)


def inverse_body(left_ref, right_ref, inverse_ref, penalty_ref):
    penalty_ref[0, 0], inverse_ref[...] = newton_inverse(left_ref[...] * right_ref[...])


def inverse_of(gram_left, gram_right):
    return pl.pallas_call(
        inverse_body,
        out_shape=(jax.ShapeDtypeStruct(gram_left.shape, f32), jax.ShapeDtypeStruct((1, 1), f32)),
        out_specs=(VM, SM),
        name="inverse",
        compiler_params=SMALL,
    )(gram_left, gram_right)


def update_body(sums_ref, start_ref, penalty_ref, inverse_ref, out_ref):
    out_ref[...] = row_update(sums_ref[...], start_ref[...], penalty_ref[0, 0], inverse_ref[...])


def update(sums, start, penalty, inverse):
    return pl.pallas_call(
        update_body,
        in_specs=[VM, VM, SM, VM],
        out_shape=jax.ShapeDtypeStruct(start.shape, bf16),
        out_specs=VM,
        name="update",
        compiler_params=SMALL,
    )(sums, start, penalty, inverse)


def second_update_body(left_ref, right_ref, sums_ref, start_ref, out_ref):
    penalty, inverse = newton_inverse(left_ref[...] * right_ref[...])
    out_ref[...] = row_update(sums_ref[...], start_ref[...], penalty, inverse)


def second_update(gram_left, gram_right, sums, start):
    return pl.pallas_call(
        second_update_body,
        out_shape=jax.ShapeDtypeStruct(start.shape, bf16),
        out_specs=VM,
        name="second_update",
        compiler_params=SMALL,
    )(gram_left, gram_right, sums, start)


def gram_body(rows_ref, out_ref):
    out_ref[...] = gram_of(rows_ref[...])


def gram_call(rows):
    return pl.pallas_call(
        gram_body,
        out_shape=jax.ShapeDtypeStruct((rows.shape[1],) * 2, f32),
        out_specs=VM,
        name="gram",
        compiler_params=SMALL,
    )(rows)


def on_device(sizes, tensor_blocks, block_coords, live_counts, factor_a, factor_b, factor_c):
    nx, ny, nz = sizes
    y_at, z_at = lax.axis_index("gy"), lax.axis_index("gz")
    slot_count, side = tensor_blocks.shape[3], tensor_blocks.shape[4]
    width = factor_a.shape[2]
    blocks = tensor_blocks.reshape(slot_count, side, side, side)
    coords = block_coords.reshape(slot_count * 3)
    live = live_counts.reshape(1)
    own_a, own_b, own_c = factor_a[0], factor_b[0], factor_c[0]
    rows_a, rows_b, rows_c = own_a.shape[0], own_b.shape[0], own_c.shape[0]
    slab = rows_a * ny * nz

    def pick(array, at, axis=0):
        return lax.dynamic_index_in_dim(array, at, axis, keepdims=False)

    def swap_cores(value):
        return lax.ppermute(value, "gz", [(0, 1), (1, 0)])

    def both_cores(value):
        other = swap_cores(value)
        return jnp.where(z_at == 0, jnp.stack([value, other]), jnp.stack([other, value]))

    def spread(value):
        sent = jnp.broadcast_to(value[None], (nx * ny,) + value.shape)
        got = lax.all_to_all(sent, ("gx", "gy"), 0, 0, tiled=True)
        return got.reshape((nx, ny) + value.shape)

    gathered = both_cores(spread(jnp.concatenate([own_b, own_c], axis=0)))
    full_b = gathered[:, :, :, :rows_b].transpose(2, 1, 0, 3, 4).reshape(ny, slab, width)
    full_c = gathered[:, :, :, rows_b:].reshape(nz, slab, width)
    slab_b = jnp.where(y_at == 0, full_b[0], full_b[1]) if ny == 2 else pick(full_b, y_at)
    slab_c = pick(full_c, z_at)

    partial, terms, own_a = contract(coords, live, blocks, slab_b, slab_c, 0, own_a)
    partial = partial.reshape(ny, nz, rows_a, width)
    sums = pick(partial, z_at, 1) + swap_cores(pick(partial, 1 - z_at, 1))
    sums = sums.reshape(ny * rows_a, width)
    gram_c, inverse, penalty = first_inverse(full_b.reshape(ny * slab, width), full_c.reshape(nz * slab, width))
    if ny == 2:
        height = ny * rows_a
        high = lax.reduce_precision(sums, 8, 7)
        sent = jnp.concatenate([high.astype(bf16), (sums - high).astype(bf16), own_a], axis=0)
        got = lax.ppermute(sent, "gy", [(0, 1), (1, 0)])
        sums = (sent[:height].astype(f32) + sent[height : 2 * height].astype(f32)) + (
            got[:height].astype(f32) + got[height : 2 * height].astype(f32)
        )
        other_a = got[2 * height :]
        start_a = jnp.where(y_at == 0, jnp.concatenate([own_a, other_a]), jnp.concatenate([other_a, own_a]))
    else:
        sums = lax.psum(sums, "gy")
        start_a = lax.all_gather(own_a, "gy", axis=0, tiled=True)
    half_a = update(sums, start_a, penalty, inverse)
    slab_a = both_cores(half_a.reshape(ny, rows_a, width)).transpose(1, 0, 2, 3).reshape(slab, width)

    inner_axes = (("gy", ny), ("gz", nz))
    partial, gram, new_a = second_contract(coords, live, blocks, terms, slab_a, slab_c, own_a, inner_axes)
    partial = partial.reshape(nx, nz, rows_b, width)
    share = width // nz
    rows_g = share // nx
    gram_part = lax.dynamic_slice_in_dim(gram, z_at * share, share, 0)
    sums = pick(partial, z_at, 1) + swap_cores(pick(partial, 1 - z_at, 1))

    def pack(sums_rows, gram_rows):
        return jnp.concatenate([sums_rows, gram_rows], axis=-2)

    def unpack(packed):
        return packed[..., :rows_b, :], packed[..., rows_b:, :]

    got = lax.all_to_all(pack(sums, gram_part.reshape(nx, rows_g, width)), "gx", 0, 0, tiled=True)
    sent = jnp.broadcast_to(jnp.sum(got, axis=0)[None], got.shape)
    gathered = both_cores(lax.all_to_all(sent, "gx", 0, 0, tiled=True))
    sums, gram_rows = unpack(gathered)
    gram_a = gram_rows.reshape(width, width)
    sums = sums.transpose(1, 0, 2, 3).reshape(slab, width)
    new_slab_b = second_update(gram_a, gram_c, sums, slab_b)
    if ny == 2:
        other_b = lax.ppermute(new_slab_b, "gy", [(0, 1), (1, 0)])
        gram_b_new = gram_call(jnp.concatenate([new_slab_b, other_b]))
    else:
        gram_b_new = gram_call(lax.all_gather(new_slab_b, "gy", axis=0, tiled=True))

    inner_axes = (("gx", nx), ("gz", nz))
    partial, new_b = contract(coords, live, blocks, slab_a, new_slab_b, 2, own_b, inner_axes)
    got = lax.all_to_all(partial.reshape(nx * ny, rows_c, width), ("gx", "gy"), 0, 0, tiled=True)
    inverse, penalty = inverse_of(gram_a, gram_b_new)
    new_c = update(jnp.sum(got.astype(f32), axis=0), own_c, penalty, inverse)
    return new_a[None], new_b[None], new_c[None]


def solution(mesh):
    sizes = tuple(mesh.shape[name] for name in ("gx", "gy", "gz"))
    return jax.shard_map(
        functools.partial(on_device, sizes),
        mesh=mesh,
        in_specs=(
            P("gx", "gy", "gz", None, None, None, None),
            P("gx", "gy", "gz", None, None),
            P("gx", "gy", "gz"),
            P("gx", ("gy", "gz"), None),
            P("gy", ("gx", "gz"), None),
            P("gz", ("gx", "gy"), None),
        ),
        out_specs=(
            P("gx", ("gy", "gz"), None),
            P("gy", ("gx", "gz"), None),
            P("gz", ("gx", "gy"), None),
        ),
        check_vma=False,
    )
```
